512 devices in a mesh: dp: 64 (over x, y, core), code: 8 (over z).
Axes of the slice: x: 4, y: 8, z: 8, core: 2. Of those that a mesh axis runs over, the one named last changes fastest.
Arguments:
- items: float32 [65536, 512], P(('dp', 'code')), may hold values from -6 to 6
- codewords: float32 [8192, 512], P('code'), may hold values from -6 to 6
- assign: int32 [65536], P('dp'), may hold values from 0 to 8191, as said below
Outputs:
- new_codewords: float32 [8192, 512], P('code', 'dp')
- residual: float32 [65536, 512], P(('dp', 'code'))
The draws below stay inside these ranges and needn't reach their ends.
Inputs may be any that keep to these rules, and one draw needn't show every extreme that they name: `assign`: the items are laid out in aligned blocks of 128 (the items of one device). Splitting the codewords into equal ranges, one per index of code, the items of one block name codewords of exactly half of the ranges, 32 items for each such range.
All inputs are finite; a program needn't handle non-finite values.
Results may differ from the reference program's by a relative error of at most 0.0003.
Values sent between devices are 32-bit elements; how exact they have to be, the bound alone decides.
No kernel may reach another device: no remote copies, remote signals or barrier semaphores. Data moves between devices by JAX's collectives and lax.ppermute only.
A program may use at most 64 MiB of HBM per device.

```python
import math
import jax
import jax.numpy as jnp
from jax import lax

D = 512
K = 8192
ROWS_DEV = 128
ITERS = 3
ITEMS = 65536
HALF_GRP = 16
N_CODE = 8


def one_block(block_key):
    first_key, second_key, third_key = jax.random.split(block_key, 3)
    ranges = jax.random.permutation(first_key, jnp.arange(N_CODE, dtype=jnp.int32))
    owner_half = ranges[jnp.arange(N_CODE, dtype=jnp.int32) // 2]
    owner_rows = jnp.repeat(owner_half, HALF_GRP)
    owner_rows = jax.random.permutation(second_key, owner_rows)
    within = jax.random.randint(third_key, (ROWS_DEV,), 0, K // N_CODE, dtype=jnp.int32)
    return owner_rows * (K // N_CODE) + within


def draw_assign(key, part):
    block_keys = jax.random.split(jax.random.fold_in(key, 17), ITEMS // ROWS_DEV)
    return jax.vmap(one_block)(block_keys).reshape(ITEMS).astype(jnp.int32)


def block_scale(key, dims, cuts, low, high):
    factor_of, own = 1.0, jax.random.fold_in(key, 6)
    for position, shards_of in cuts:
        draws = jnp.exp(jax.random.uniform(jax.random.fold_in(own, position), (shards_of,), jnp.float32, low / len(cuts), high / len(cuts)))
        factor_of = factor_of * jnp.repeat(draws, dims[position] // shards_of).reshape([-1 if axis == position else 1 for axis in range(len(dims))])
    return factor_of


def bell_draw(stream_key, extent, spread, most, cuts=(), kind=jnp.bfloat16):
    gain = block_scale(stream_key, extent, cuts, -0.22, 0.18) if cuts else 1.0
    drawn = jax.random.normal(stream_key, extent, jnp.float32) * spread * gain
    return jnp.minimum(jnp.maximum(drawn, -most), most).astype(kind)


def setup_inputs(seed: int = 0) -> dict:
    keys = jax.random.split(jax.random.key(seed), 4)
    items = bell_draw(keys[0], (ITEMS, D), 1.0, 6.0, ((0, 512),), jnp.float32)
    codewords = bell_draw(keys[1], (K, D), 1.0, 6.0, ((0, 8),), jnp.float32)
    assign = draw_assign(jax.random.fold_in(keys[3], 71), 0)
    return {"items": items, "codewords": codewords, "assign": assign}


epsilon = 1e-05
inverse_temp = 64.0

def unit_rows(values):
    return values * lax.rsqrt(lax.optimization_barrier(jnp.mean(values * values, axis=-1, keepdims=True)) + epsilon)

def reference(items, codewords, assign):
    scaled = unit_rows(codewords) * (inverse_temp / D)
    block = math.gcd(ITEMS, 1024)
    item_blocks = items.reshape(ITEMS // block, block, D)

    def kernel_of(rows_block):
        return jnp.exp(jnp.dot(unit_rows(rows_block), scaled.T, precision=lax.Precision.HIGHEST, preferred_element_type=jnp.float32))

    def first_sweep(col_acc, rows_block):
        return (col_acc + lax.optimization_barrier(jnp.sum(kernel_of(rows_block), axis=0)), None)
    col_part, _ = lax.scan(first_sweep, jnp.zeros((K,), jnp.float32), item_blocks)
    numerator = jnp.zeros((K, D), jnp.float32)
    for sweep_index in range(ITERS):
        col_scale = 1.0 / (K * col_part)
        final_turn = sweep_index == ITERS - 1

        def sweep(carry, rows_block):
            col_acc, numer_acc = carry
            kernel_block = kernel_of(rows_block)
            row_part = jnp.dot(kernel_block, col_scale, precision=lax.Precision.HIGHEST, preferred_element_type=jnp.float32)
            row_scale = 1.0 / (ITEMS * row_part)
            col_acc = col_acc + jnp.dot(row_scale, kernel_block, precision=lax.Precision.HIGHEST, preferred_element_type=jnp.float32)
            if final_turn:
                numer_acc = numer_acc + jnp.dot(kernel_block.T, row_scale[:, None] * rows_block, precision=lax.Precision.HIGHEST, preferred_element_type=jnp.float32)
            return ((col_acc, numer_acc), None)
        (col_part, numerator), _ = lax.scan(sweep, (jnp.zeros((K,), jnp.float32), jnp.zeros((K, D), jnp.float32)), item_blocks)
    new_codewords = numerator / col_part[:, None]
    residual = items - jnp.take(codewords, assign.astype(jnp.int32), axis=0)
    return (new_codewords, residual)
```

```python
import jax
import jax.numpy as jnp
from jax import lax
from jax.sharding import Mesh, PartitionSpec as P

K = 8192
ITERS = 3
DP = ("x", "y", "core")

epsilon = 1e-05
inverse_temp = 64.0


def unit_rows(values):
    return values * lax.rsqrt(jnp.mean(values * values, axis=-1, keepdims=True) + epsilon)


def exchange_sum(part, axes):
    count = lax.axis_size(axes)
    copies = jnp.broadcast_to(part[None], (count,) + part.shape)
    return jnp.sum(lax.all_to_all(copies, axes, 0, 0), axis=0)


def scatter_sum(blocks, axis):
    return jnp.sum(lax.all_to_all(blocks, axis, 0, 0), axis=0)


def body(items, codewords, assign):
    code_count = lax.axis_size("code")
    dp_count = lax.axis_size(DP)
    local_codes = codewords.shape[0]
    own_rows, width = items.shape
    total_items = own_rows * code_count * dp_count
    scaled = unit_rows(codewords) * (inverse_temp / width)
    gathered = lax.all_gather(items, "code", axis=0, tiled=True)
    logits = lax.dot_general(
        unit_rows(gathered),
        scaled,
        (((1,), (1,)), ((), ())),
        precision=lax.Precision.HIGH,
        preferred_element_type=jnp.float32,
    )
    kernel_vals = jnp.exp(logits)
    col_part = jnp.sum(kernel_vals, axis=0)
    for _ in range(ITERS):
        col_scale = 1.0 / (K * exchange_sum(col_part, DP))
        row_part = jnp.sum(kernel_vals * col_scale[None, :], axis=1)
        row_scale = 1.0 / (total_items * exchange_sum(row_part, "code"))
        col_part = jnp.sum(kernel_vals * row_scale[:, None], axis=0)
    mass = exchange_sum(col_part, DP)

    nx, ny, nc = lax.axis_size("x"), lax.axis_size("y"), lax.axis_size("core")
    cols = width // dp_count
    numerator = lax.dot_general(
        row_scale[:, None] * gathered,
        kernel_vals,
        (((0,), (0,)), ((), ())),
        precision=lax.Precision.HIGH,
        preferred_element_type=jnp.float32,
    )
    halves = numerator.reshape(nx * ny, nc, cols, local_codes)
    core = lax.axis_index("core")
    mine = lax.dynamic_index_in_dim(halves, core, 1, keepdims=False)
    other = lax.dynamic_index_in_dim(halves, 1 - core, 1, keepdims=False)
    chip = mine + lax.ppermute(other, "core", [(0, 1), (1, 0)])
    owned = scatter_sum(chip.reshape(nx, ny, cols, local_codes), "x")
    owned = scatter_sum(owned, "y")
    new_codewords = (owned / mass[None, :]).T

    my_code = lax.axis_index("code")
    offset = my_code * local_codes
    index_rows = assign - offset
    inside = (index_rows >= 0) & (index_rows < local_codes)
    picked = jnp.take(codewords, jnp.clip(index_rows, 0, local_codes - 1), axis=0)
    looked = lax.psum_scatter(
        jnp.where(inside[:, None], picked, jnp.float32(0.0)),
        "code",
        scatter_dimension=0,
        tiled=True,
    )
    residual = items - looked
    return (new_codewords, residual)


def solution(mesh):
    cores = 2
    ny = 8
    dp, code = mesh.devices.shape
    fine = Mesh(
        mesh.devices.reshape(dp // (ny * cores), ny, cores, code),
        ("x", "y", "core", "code"),
    )
    in_specs = (P(DP + ("code",), None), P("code", None), P(DP))
    out_specs = (P("code", DP), P(DP + ("code",), None))
    return jax.shard_map(body, mesh=fine, in_specs=in_specs, out_specs=out_specs, check_vma=False)
```

```python
import functools

import jax
import jax.numpy as jnp
from jax import lax
from jax.experimental import pallas as pl
from jax.experimental.pallas import tpu as pltpu
from jax.sharding import Mesh, PartitionSpec as P

K = 8192
ITERS = 3
DP = ("x", "y", "core")
LANES = 128
SUB = 8

epsilon = 1e-05
inverse_temp = 64.0

VMEM = pl.BlockSpec(memory_space=pltpu.VMEM)
SMEM = pl.BlockSpec(memory_space=pltpu.SMEM)
MIB = 1024 * 1024


def call(body, out_shape, ins, scratch=(), grant=8):
    return pl.pallas_call(
        body,
        out_shape=out_shape,
        in_specs=ins,
        out_specs=jax.tree.map(lambda _: VMEM, out_shape),
        scratch_shapes=list(scratch),
        compiler_params=pltpu.CompilerParams(vmem_limit_bytes=grant * MIB),
    )


def split(values):
    high = values.astype(jnp.bfloat16)
    return high, (values - high.astype(jnp.float32)).astype(jnp.bfloat16)


def unit_rows(values):
    return values * lax.rsqrt(jnp.mean(values * values, axis=-1, keepdims=True) + epsilon)


def dot_nt(a, b):
    return lax.dot_general(a, b, (((1,), (1,)), ((), ())), preferred_element_type=jnp.float32)


def lane_sums(block):
    return jnp.sum(block.T, axis=0, keepdims=True)


def scale_kernel(codes_ref, high_ref, low_ref):
    width = codes_ref.shape[1]
    high, low = split(unit_rows(codes_ref[...]) * (inverse_temp / width))
    high_ref[...] = high
    low_ref[...] = low


def chunk_kernel(count, high_ref, low_ref, *refs):
    item_refs, (out_ref, sums_ref, th_ref, tl_ref) = refs[:count], refs[count:]
    rows = item_refs[0].shape[0]
    width = item_refs[0].shape[1]
    highs, lows = [], []
    for j, ref in enumerate(item_refs):
        values = ref[...]
        high, low = split(unit_rows(values))
        highs.append(high)
        lows.append(low)
        turned = values.T.reshape(width // (2 * SUB), 2, SUB, rows)
        for core in range(2):
            half_high, half_low = split(turned[:, core].reshape(width // 2, rows))
            th_ref[core, :, j * rows:(j + 1) * rows] = half_high
            tl_ref[core, :, j * rows:(j + 1) * rows] = half_low
    item_high = jnp.concatenate(highs, axis=0) if count > 1 else highs[0]
    item_low = jnp.concatenate(lows, axis=0) if count > 1 else lows[0]
    codes = high_ref.shape[0]
    step = 256
    for start in range(0, codes, step):
        code_high = high_ref[start:start + step]
        code_low = low_ref[start:start + step]
        logits = dot_nt(code_high, item_high) + (dot_nt(code_high, item_low) + dot_nt(code_low, item_high))
        values = jnp.exp(logits)
        out_ref[start:start + step] = values
        folded = values[:, :rows]
        for j in range(1, count):
            folded = folded + values[:, j * rows:(j + 1) * rows]
        for part in range(step // LANES):
            row = start // LANES + part
            sums_ref[row:row + 1] = lane_sums(folded[part * LANES:(part + 1) * LANES])


def load_blocks(refs):
    return [(ref, j * LANES) for ref in refs for j in range(ref.shape[1] // LANES)]


def row_kernel(order, z_ref, got_ref, *refs):
    blocks, out_ref = load_blocks(refs[:-1]), refs[-1]
    scale = 1.0 / (K * jnp.sum(got_ref[...], axis=0))
    totals = [jnp.zeros((SUB, LANES), jnp.float32) for _ in blocks]
    for b in range(scale.shape[0]):
        column = jnp.broadcast_to(scale[b:b + 1], (LANES, LANES)).T
        for j, (ref, lane) in enumerate(blocks):
            product = ref[b * LANES:(b + 1) * LANES, lane:lane + LANES] * column
            totals[j] = totals[j] + jnp.sum(product.reshape(LANES // SUB, SUB, LANES), axis=0)
    rows = [None] * len(blocks)
    for j, offset in enumerate(order):
        rows[offset] = jnp.sum(totals[j], axis=0, keepdims=True)
    tile = pltpu.roll(jnp.concatenate(rows, axis=0), z_ref[0], 0)
    for peer in range(out_ref.shape[0]):
        out_ref[peer] = tile


def row_scales(order, total_items, z_ref, got_ref):
    scale = 1.0 / (total_items * jnp.sum(got_ref[...], axis=0))
    tile = pltpu.roll(scale, z_ref[1], 0)
    return [tile[offset:offset + 1] for offset in order]


def col_kernel(order, total_items, z_ref, got_ref, *refs):
    blocks, out_ref = load_blocks(refs[:-1]), refs[-1]
    scales = row_scales(order, total_items, z_ref, got_ref)
    for b in range(out_ref.shape[0]):
        folded = jnp.zeros((LANES, LANES), jnp.float32)
        for (ref, lane), scale in zip(blocks, scales):
            folded = folded + ref[b * LANES:(b + 1) * LANES, lane:lane + LANES] * scale
        out_ref[b:b + 1] = lane_sums(folded)


def numer_kernel(order, total_items, count, nx, ny, z_ref, got_ref, *refs):
    blocks = load_blocks(refs[:count])
    high_refs, low_refs = refs[count:2 * count], refs[2 * count:3 * count]
    out_ref, wh_ref, wl_ref, xh_ref, xl_ref = refs[3 * count:]
    scales = row_scales(order, total_items, z_ref, got_ref)
    lane, half = 0, xh_ref.shape[0] // 2
    for high, low in zip(high_refs, low_refs):
        size = high.shape[2]
        for core in range(2):
            xh_ref[core * half:(core + 1) * half, lane:lane + size] = high[core]
            xl_ref[core * half:(core + 1) * half, lane:lane + size] = low[core]
        lane += size
    codes = refs[0].shape[0]
    step = 256
    mass = []
    for start in range(0, codes, step):
        for part in range(step // LANES):
            top = start + part * LANES
            folded = jnp.zeros((LANES, LANES), jnp.float32)
            for j, ((ref, lane), scale) in enumerate(zip(blocks, scales)):
                weights = ref[top:top + LANES, lane:lane + LANES] * scale
                folded = folded + weights
                high, low = split(weights)
                wh_ref[part * LANES:(part + 1) * LANES, j * LANES:(j + 1) * LANES] = high
                wl_ref[part * LANES:(part + 1) * LANES, j * LANES:(j + 1) * LANES] = low
            mass.append(lane_sums(folded))
        weight_high, weight_low = wh_ref[...], wl_ref[...]
        sums = dot_nt(xh_ref[...], weight_high) + (dot_nt(xh_ref[...], weight_low) + dot_nt(xl_ref[...], weight_high))
        for core in range(2):
            slot = jnp.where(z_ref[2] == core, 0, 1)
            for part in range(step // LANES):
                col = start // LANES + part
                for x in range(nx):
                    for y in range(ny):
                        row = core * half + (x * ny + y) * SUB
                        out_ref[slot, x, y * SUB + col] = sums[row:row + SUB, part * LANES:(part + 1) * LANES]
    tile = jnp.concatenate(mass, axis=0)
    for core in range(2):
        for x in range(nx):
            out_ref[core, x, ny * SUB] = tile


def repack_kernel(got_ref, out_ref):
    summed = got_ref[0]
    for x in range(1, got_ref.shape[0]):
        summed = summed + got_ref[x]
    ny, count = out_ref.shape[0], out_ref.shape[1]
    for y in range(ny):
        out_ref[y, :count - 1] = summed[y * (count - 1):(y + 1) * (count - 1)]
        out_ref[y, count - 1] = summed[ny * (count - 1)]


def finish_kernel(got_ref, out_ref):
    summed = jnp.sum(got_ref[...], axis=0)
    count = summed.shape[0] - 1
    for b in range(count):
        out_ref[:, b * LANES:(b + 1) * LANES] = summed[b] / summed[count][b:b + 1]


def body(items, codewords, assign):
    f32 = jnp.float32
    code_count = lax.axis_size("code")
    nx, ny, nc = lax.axis_size("x"), lax.axis_size("y"), lax.axis_size("core")
    local_codes, width = codewords.shape
    own_rows = items.shape[0]
    total_items = own_rows * code_count * nx * ny * nc
    my_code = lax.axis_index("code")
    z_info = jnp.stack([my_code, lax.rem(code_count - my_code, code_count), lax.axis_index("core")]).astype(jnp.int32)

    items, z_info = lax.optimization_barrier((items, z_info))

    half = jax.ShapeDtypeStruct((local_codes, width), jnp.bfloat16)
    code_high, code_low = call(scale_kernel, (half, half), [VMEM])(codewords)

    def chunk(*arrived):
        count = len(arrived)
        lanes = count * own_rows
        turned = jax.ShapeDtypeStruct((2, width // 2, lanes), jnp.bfloat16)
        shapes = (
            jax.ShapeDtypeStruct((local_codes, lanes), f32),
            jax.ShapeDtypeStruct((local_codes // LANES, LANES), f32),
            turned,
            turned,
        )
        return call(functools.partial(chunk_kernel, count), shapes, [VMEM] * (2 + count))(code_high, code_low, *arrived)

    index_rows = assign - my_code * local_codes
    inside = (index_rows >= 0) & (index_rows < local_codes)
    picked = jnp.take(codewords, jnp.clip(index_rows, 0, local_codes - 1), axis=0)
    named = jnp.where(inside[:, None], picked, jnp.float32(0.0))

    up = [(i, (i + 1) % code_count) for i in range(code_count)]
    down = [(i, (i - 1) % code_count) for i in range(code_count)]
    chunks, order = [chunk(items)], [0]
    right = left = items
    for step in range(1, code_count // 2 + 1):
        right = lax.ppermute(right, "code", up)
        if step < code_count // 2:
            if step == 2:
                named, left = lax.optimization_barrier((named, left))
            left, chunks[step - 1] = lax.optimization_barrier((left, chunks[step - 1]))
            left = lax.ppermute(left, "code", down)
            chunks.append(chunk(right, left))
            order += [code_count - step, step]
        else:
            chunks.append(chunk(right))
            order += [code_count - step]
    blocks = [c[0] for c in chunks]
    count = len(blocks)
    col_tile = sum(c[1] for c in chunks)

    def over_items(tile):
        chip = tile + lax.ppermute(tile, "core", [(0, 1), (1, 0)])
        return lax.all_to_all(jnp.broadcast_to(chip[None], (nx * ny,) + chip.shape), ("x", "y"), 0, 0)

    row_shape = jax.ShapeDtypeStruct((code_count, SUB, LANES), f32)
    col_shape = jax.ShapeDtypeStruct((local_codes // LANES, LANES), f32)
    operands = [SMEM, VMEM] + [VMEM] * count
    for turn in range(ITERS):
        got = over_items(col_tile)
        rows = call(functools.partial(row_kernel, order), row_shape, operands)(z_info, got, *blocks)
        if turn == 0:
            named, rows = lax.optimization_barrier((named, rows))
            looked = lax.psum_scatter(named, "code", scatter_dimension=0, tiled=True)
        got = lax.all_to_all(rows, "code", 0, 0)
        if turn < ITERS - 1:
            col_tile = call(functools.partial(col_kernel, order, total_items), col_shape, operands)(z_info, got, *blocks)

    tiles = jax.ShapeDtypeStruct((nc, nx, ny * SUB + 1, SUB, LANES), f32)
    numer = call(
        functools.partial(numer_kernel, order, total_items, count, nx, ny),
        tiles,
        operands + [VMEM] * (2 * count),
        [pltpu.VMEM((256, own_rows * code_count), jnp.bfloat16)] * 2
        + [pltpu.VMEM((width, own_rows * code_count), jnp.bfloat16)] * 2,
        grant=16,
    )(z_info, got, *blocks, *[c[2] for c in chunks], *[c[3] for c in chunks])
    partner = lax.ppermute(numer[1], "core", [(0, 1), (1, 0)])
    partner, residual = lax.optimization_barrier((partner, items - looked))
    chip = numer[0] + partner
    got = lax.all_to_all(chip, "x", 0, 0)
    packed = call(repack_kernel, jax.ShapeDtypeStruct((ny, SUB + 1, SUB, LANES), f32), [VMEM])(got)
    got = lax.all_to_all(packed, "y", 0, 0)
    turned = call(finish_kernel, jax.ShapeDtypeStruct((width // (nx * ny * nc), local_codes), f32), [VMEM])(got)
    new_codewords = turned.T

    return (new_codewords, residual)


def solution(mesh):
    cores = 2
    ny = 8
    dp, code = mesh.devices.shape
    fine = Mesh(
        mesh.devices.reshape(dp // (ny * cores), ny, cores, code),
        ("x", "y", "core", "code"),
    )
    in_specs = (P(DP + ("code",), None), P("code", None), P(DP))
    out_specs = (P("code", DP), P(DP + ("code",), None))
    return jax.shard_map(body, mesh=fine, in_specs=in_specs, out_specs=out_specs, check_vma=False)
```

```python
import functools

import jax
import jax.numpy as jnp
from jax import lax
from jax.experimental import pallas as pl
from jax.experimental.pallas import tpu as pltpu
from jax.sharding import Mesh, PartitionSpec as P

K = 8192
ITERS = 3
DP = ("x", "y", "core")
LANES = 128
SUB = 8

epsilon = 1e-05
inverse_temp = 64.0

VMEM = pl.BlockSpec(memory_space=pltpu.VMEM)
SMEM = pl.BlockSpec(memory_space=pltpu.SMEM)
MIB = 1024 * 1024


def call(body, out_shape, ins, scratch=(), grant=8):
    return pl.pallas_call(
        body,
        out_shape=out_shape,
        in_specs=ins,
        out_specs=jax.tree.map(lambda _: VMEM, out_shape),
        scratch_shapes=list(scratch),
        compiler_params=pltpu.CompilerParams(vmem_limit_bytes=grant * MIB),
    )


def split(values):
    high = values.astype(jnp.bfloat16)
    return high, (values - high.astype(jnp.float32)).astype(jnp.bfloat16)


def unit_rows(values):
    return values * lax.rsqrt(jnp.mean(values * values, axis=-1, keepdims=True) + epsilon)


def dot_nt(a, b):
    return lax.dot_general(a, b, (((1,), (1,)), ((), ())), preferred_element_type=jnp.float32)


def lane_sums(block):
    return jnp.sum(block.T, axis=0, keepdims=True)


def scale_kernel(z_ref, codes_ref, high_ref, low_ref):
    half, width = high_ref.shape
    codes = codes_ref[pl.ds(pl.multiple_of(z_ref[2] * half, half), half)]
    high, low = split(unit_rows(codes) * (inverse_temp / width))
    high_ref[...] = high
    low_ref[...] = low


def pair_kernel(z_ref, own_ref, other_ref, out_ref):
    out_ref[z_ref[2]] = own_ref[...]
    out_ref[1 - z_ref[2]] = other_ref[...]


def chunk_kernel(count, high_ref, low_ref, *refs):
    item_refs, (out_ref, sums_ref, xh_ref, xl_ref) = refs[:count], refs[count:]
    rows = item_refs[0].shape[0] * item_refs[0].shape[1]
    width = item_refs[0].shape[2]
    highs, lows = [], []
    for j, ref in enumerate(item_refs):
        values = ref[...].reshape(rows, width)
        high, low = split(unit_rows(values))
        highs.append(high)
        lows.append(low)
        xh_ref[j * rows:(j + 1) * rows], xl_ref[j * rows:(j + 1) * rows] = split(values)
    codes = high_ref.shape[0]
    step = 256
    for start in range(0, codes, step):
        code_high = high_ref[start:start + step]
        code_low = low_ref[start:start + step]
        folded = jnp.zeros((step, LANES), jnp.float32)
        for j, (item_high, item_low) in enumerate(zip(highs, lows)):
            logits = dot_nt(code_high, item_high) + (dot_nt(code_high, item_low) + dot_nt(code_low, item_high))
            values = jnp.exp(logits)
            out_ref[start:start + step, j * rows:(j + 1) * rows] = values
            for lane in range(0, rows, LANES):
                folded = folded + values[:, lane:lane + LANES]
        for part in range(step // LANES):
            row = start // LANES + part
            sums_ref[row:row + 1] = lane_sums(folded[part * LANES:(part + 1) * LANES])


def load_blocks(refs):
    return [(ref, j * LANES) for ref in refs for j in range(ref.shape[1] // LANES)]


def row_kernel(orders, z_ref, got_ref, *refs):
    blocks, out_ref = load_blocks(refs[:-1]), refs[-1]
    scale = 1.0 / (K * jnp.sum(got_ref[...], axis=0))
    totals = [jnp.zeros((SUB, LANES), jnp.float32) for _ in blocks]
    for b in range(scale.shape[0]):
        column = jnp.broadcast_to(scale[b:b + 1], (LANES, LANES)).T
        for j, (ref, lane) in enumerate(blocks):
            product = ref[b * LANES:(b + 1) * LANES, lane:lane + LANES] * column
            totals[j] = totals[j] + jnp.sum(product.reshape(LANES // SUB, SUB, LANES), axis=0)
    sums = [jnp.sum(total, axis=0, keepdims=True) for total in totals]
    tiles = []
    for order in orders:
        rows = [None] * len(blocks)
        for j, place in enumerate(order):
            rows[place] = sums[j]
        tiles.append(jnp.concatenate(rows, axis=0))
    tile = pltpu.roll(jnp.where(z_ref[2] == 0, tiles[0], tiles[1]), z_ref[0], 0)
    for peer in range(out_ref.shape[0]):
        out_ref[peer] = tile


def row_scales(orders, total_items, z_ref, got_ref):
    scale = 1.0 / (total_items * jnp.sum(got_ref[...], axis=0))
    tile = pltpu.roll(scale, z_ref[1], 0)
    return [jnp.where(z_ref[2] == 0, tile[a:a + 1], tile[b:b + 1]) for a, b in zip(*orders)]


def col_kernel(orders, total_items, z_ref, got_ref, *refs):
    blocks, out_ref = load_blocks(refs[:-1]), refs[-1]
    scales = row_scales(orders, total_items, z_ref, got_ref)
    rows = []
    for b in range(out_ref.shape[1]):
        folded = jnp.zeros((LANES, LANES), jnp.float32)
        for (ref, lane), scale in zip(blocks, scales):
            folded = folded + ref[b * LANES:(b + 1) * LANES, lane:lane + LANES] * scale
        rows.append(lane_sums(folded))
    tile = jnp.concatenate(rows, axis=0)
    for peer in range(out_ref.shape[0]):
        out_ref[peer] = tile


def numer_kernel(orders, total_items, count, z_ref, got_ref, *refs):
    high_refs, low_refs, out_ref = refs[count:2 * count], refs[2 * count:3 * count], refs[3 * count]
    scales = row_scales(orders, total_items, z_ref, got_ref)
    codes, width = refs[0].shape[0], high_refs[0].shape[1]
    nx = out_ref.shape[0]
    parts = codes // LANES
    step = 256
    mass = []
    for start in range(0, codes, step):
        folded = jnp.zeros((step, LANES), jnp.float32)
        sums, at = None, 0
        for ref, xh_ref, xl_ref in zip(refs[:count], high_refs, low_refs):
            highs, lows = [], []
            for lane in range(0, ref.shape[1], LANES):
                weights = ref[start:start + step, lane:lane + LANES] * scales[at]
                folded = folded + weights
                high, low = split(weights)
                highs.append(high)
                lows.append(low)
                at += 1
            high, low = jnp.concatenate(highs, axis=1), jnp.concatenate(lows, axis=1)
            xh, xl = xh_ref[...], xl_ref[...]
            more = jnp.dot(high, xh, preferred_element_type=jnp.float32) + (
                jnp.dot(low, xh, preferred_element_type=jnp.float32)
                + jnp.dot(high, xl, preferred_element_type=jnp.float32)
            )
            sums = more if sums is None else sums + more
        for part in range(step // LANES):
            mass.append(lane_sums(folded[part * LANES:(part + 1) * LANES]))
            col = start // LANES + part
            for x in range(nx):
                for lane in range(x * width // nx, (x + 1) * width // nx, LANES):
                    turned = sums[part * LANES:(part + 1) * LANES, lane:lane + LANES].T
                    for group in range(LANES // SUB):
                        row = (lane - x * width // nx) // SUB + group
                        out_ref[x, row * parts + col] = turned[group * SUB:(group + 1) * SUB]
    tile = jnp.concatenate(mass + [jnp.ones((SUB - parts, LANES), jnp.float32)], axis=0)
    for x in range(nx):
        out_ref[x, out_ref.shape[1] - 1] = tile


def repack_kernel(got_ref, out_ref):
    summed = got_ref[0]
    for x in range(1, got_ref.shape[0]):
        summed = summed + got_ref[x]
    ny, count = out_ref.shape[0], out_ref.shape[1]
    for y in range(ny):
        out_ref[y, :count - 1] = summed[y * (count - 1):(y + 1) * (count - 1)]
        out_ref[y, count - 1] = summed[ny * (count - 1)]


def lookup_kernel(first, z_ref, index_ref, codes_ref, *refs):
    out_ref, start = refs[-1], 0
    if len(refs) > 1:
        start = refs[0].shape[0]
        out_ref[:start] = refs[0][...]
    part0 = codes_ref[...].astype(jnp.bfloat16)
    rest = codes_ref[...] - part0.astype(jnp.float32)
    part1 = rest.astype(jnp.bfloat16)
    part2 = (rest - part1.astype(jnp.float32)).astype(jnp.bfloat16)
    codes = codes_ref.shape[0]
    for block in range((out_ref.shape[0] - start) // LANES):
        local = index_ref[first + block:first + block + 1] - z_ref[3]
        column = jnp.broadcast_to(local.astype(jnp.float32), (LANES, LANES)).T
        hits = []
        for b in range(codes // LANES):
            lane = lax.broadcasted_iota(jnp.int32, (LANES, LANES), 1) + b * LANES
            hits.append(jnp.where(column == lane.astype(jnp.float32), 1.0, 0.0).astype(jnp.bfloat16))
        chosen = jnp.concatenate(hits, axis=1)
        found = jnp.dot(chosen, part2, preferred_element_type=jnp.float32)
        found = jnp.dot(chosen, part1, preferred_element_type=jnp.float32) + found
        found = jnp.dot(chosen, part0, preferred_element_type=jnp.float32) + found
        out_ref[start + block * LANES:start + (block + 1) * LANES] = found


def finish_kernel(z_ref, got_ref, items_ref, looked_ref, out_ref, residual_ref):
    residual_ref[...] = items_ref[...] - looked_ref[...]
    summed = jnp.sum(got_ref[...], axis=0)
    count = summed.shape[0] - 1
    parts = count // 2
    for core in range(2):
        slot = jnp.where(z_ref[2] == core, 0, 1)
        for b in range(parts):
            out_ref[slot, :, b * LANES:(b + 1) * LANES] = summed[core * parts + b] / summed[count][b:b + 1]


def body(items, codewords, assign):
    f32 = jnp.float32
    n = lax.axis_size("code")
    nx, ny, nc = lax.axis_size("x"), lax.axis_size("y"), lax.axis_size("core")
    local_codes, width = codewords.shape
    own_rows = items.shape[0]
    pair_rows = nc * own_rows
    half = local_codes // nc
    total_items = pair_rows * n * nx * ny
    my_code = lax.axis_index("code")
    core = lax.axis_index("core")
    shift = nc * my_code
    z_info = jnp.stack([shift, lax.rem(nc * n - shift, nc * n), core, my_code * local_codes]).astype(jnp.int32)
    items, z_info = lax.optimization_barrier((items, z_info))
    swap = [(0, 1), (1, 0)]

    other = lax.ppermute(items, "core", swap)
    scaled = jax.ShapeDtypeStruct((half, width), jnp.bfloat16)
    code_high, code_low = call(scale_kernel, (scaled, scaled), [SMEM, VMEM])(z_info, codewords)
    pair = call(pair_kernel, jax.ShapeDtypeStruct((nc,) + items.shape, f32), [SMEM, VMEM, VMEM])(z_info, items, other)

    def chunk(*arrived):
        count = len(arrived)
        lanes = count * pair_rows
        parts = jax.ShapeDtypeStruct((lanes, width), jnp.bfloat16)
        shapes = (
            jax.ShapeDtypeStruct((half, lanes), f32),
            jax.ShapeDtypeStruct((half // LANES, LANES), f32),
            parts,
            parts,
        )
        return call(functools.partial(chunk_kernel, count), shapes, [VMEM] * (2 + count))(code_high, code_low, *arrived)

    index_tile = assign.reshape(-1, LANES)
    piece = index_tile.shape[0] // 2

    def lookup(first, *before):
        rows = piece * LANES * (1 + len(before))
        shape = jax.ShapeDtypeStruct((rows, width), f32)
        operands = [SMEM] + [VMEM] * (2 + len(before))
        return call(functools.partial(lookup_kernel, first), shape, operands, grant=12)(
            z_info, index_tile, codewords, *before
        )

    around = [(i, (i + 1) % n) for i in range(n)] + [(n + i, n + (i - 1) % n) for i in range(n)]
    last = n // 2
    chunks, places = [chunk(pair)], [0]
    came = pair
    named = None
    for step in range(1, last + 1):
        before = came
        came = lax.ppermute(came, ("core", "code"), around)
        if step > 1:
            handed = lax.ppermute(before, "core", swap)
            if step == 2:
                named = lookup(0)
                handed, named = lax.optimization_barrier((handed, named))
            elif step == 3:
                named = lookup(piece, named)
                handed, named = lax.optimization_barrier((handed, named))
            chunks.append(chunk(before, handed))
            places += [n - step + 1, step - 1]
        came, chunks[-1] = lax.optimization_barrier((came, chunks[-1]))
    chunks.append(chunk(came))
    places += [last]
    flipped = [(n - place) % n for place in places]
    orders = [[nc * place + c for place in order for c in range(nc)] for order in (places, flipped)]
    blocks = [c[0] for c in chunks]
    count = len(blocks)
    col_tile, named = lax.optimization_barrier((sum(c[1] for c in chunks), named))
    looked = lax.psum_scatter(named, "code", scatter_dimension=0, tiled=True)

    row_shape = jax.ShapeDtypeStruct((nc * n, nc * n, LANES), f32)
    col_shape = jax.ShapeDtypeStruct((nx * ny,) + col_tile.shape, f32)
    operands = [SMEM, VMEM] + [VMEM] * count
    cols = jnp.broadcast_to(col_tile[None], col_shape.shape)
    for turn in range(ITERS):
        got = lax.all_to_all(cols, ("x", "y"), 0, 0)
        rows = call(functools.partial(row_kernel, orders), row_shape, operands)(z_info, got, *blocks)
        got = lax.all_to_all(rows, ("core", "code"), 0, 0)
        if turn < ITERS - 1:
            cols = call(functools.partial(col_kernel, orders, total_items), col_shape, operands)(z_info, got, *blocks)

    per_owner = width // (nx * ny * nc)
    tiles = ny * nc * (per_owner // SUB) * (half // LANES)
    numer = call(
        functools.partial(numer_kernel, orders, total_items, count),
        jax.ShapeDtypeStruct((nx, tiles + 1, SUB, LANES), f32),
        operands + [VMEM] * (2 * count),
        grant=16,
    )(z_info, got, *blocks, *[c[2] for c in chunks], *[c[3] for c in chunks])
    got = lax.all_to_all(numer, "x", 0, 0)
    got, looked = lax.optimization_barrier((got, looked))
    packed = call(repack_kernel, jax.ShapeDtypeStruct((ny, tiles // ny + 1, SUB, LANES), f32), [VMEM])(got)
    got = lax.all_to_all(packed, "y", 0, 0)
    shapes = (jax.ShapeDtypeStruct((nc, per_owner, half), f32), jax.ShapeDtypeStruct(items.shape, f32))
    turned, residual = call(finish_kernel, shapes, [SMEM] + [VMEM] * 3)(z_info, got, items, looked)
    mine, given = turned[0], lax.ppermute(turned[1], "core", swap)
    new_codewords = jnp.concatenate([jnp.where(core == 0, mine, given), jnp.where(core == 0, given, mine)], axis=1).T
    return (new_codewords, residual)


def solution(mesh):
    cores = 2
    ny = 8
    dp, code = mesh.devices.shape
    fine = Mesh(
        mesh.devices.reshape(dp // (ny * cores), ny, cores, code),
        ("x", "y", "core", "code"),
    )
    in_specs = (P(DP + ("code",), None), P("code", None), P(DP))
    out_specs = (P("code", DP), P(DP + ("code",), None))
    return jax.shard_map(body, mesh=fine, in_specs=in_specs, out_specs=out_specs, check_vma=False)
```

```python
import functools

import jax
import jax.numpy as jnp
from jax import lax
from jax.experimental import pallas as pl
from jax.experimental.pallas import tpu as pltpu
from jax.sharding import Mesh, PartitionSpec as P

K = 8192
ITERS = 3
DP = ("x", "y", "core")
LANES = 128
SUB = 8

epsilon = 1e-05
inverse_temp = 64.0

VMEM = pl.BlockSpec(memory_space=pltpu.VMEM)
SMEM = pl.BlockSpec(memory_space=pltpu.SMEM)
MIB = 1024 * 1024


def call(body, out_shape, ins, scratch=(), grant=8):
    return pl.pallas_call(
        body,
        out_shape=out_shape,
        in_specs=ins,
        out_specs=jax.tree.map(lambda _: VMEM, out_shape),
        scratch_shapes=list(scratch),
        compiler_params=pltpu.CompilerParams(vmem_limit_bytes=grant * MIB),
    )


def split(values):
    high = values.astype(jnp.bfloat16)
    return high, (values - high.astype(jnp.float32)).astype(jnp.bfloat16)


def unit_rows(values):
    return values * lax.rsqrt(jnp.mean(values * values, axis=-1, keepdims=True) + epsilon)


def dot_nt(a, b):
    return lax.dot_general(a, b, (((1,), (1,)), ((), ())), preferred_element_type=jnp.float32)


def lane_sums(block):
    return jnp.sum(block.T, axis=0, keepdims=True)


def scale_kernel(z_ref, codes_ref, high_ref, low_ref):
    half, width = high_ref.shape
    codes = codes_ref[pl.ds(pl.multiple_of(z_ref[0] * half, half), half)]
    high, low = split(unit_rows(codes) * (inverse_temp / width))
    high_ref[...] = high
    low_ref[...] = low


def chunk_kernel(high_ref, low_ref, items_ref, out_ref, sums_ref, xh_ref, xl_ref):
    codes, step = high_ref.shape[0], 256
    folded = [jnp.zeros((step, LANES), jnp.float32) for _ in range(0, codes, step)]
    for first in range(0, items_ref.shape[0], step):
        values = items_ref[first:first + step]
        xh_ref[first:first + step], xl_ref[first:first + step] = split(values)
        item_high, item_low = split(unit_rows(values))
        for k, start in enumerate(range(0, codes, step)):
            code_high = high_ref[start:start + step]
            code_low = low_ref[start:start + step]
            logits = dot_nt(code_high, item_high) + (dot_nt(code_high, item_low) + dot_nt(code_low, item_high))
            values = jnp.exp(logits)
            out_ref[start:start + step, first:first + step] = values
            for lane in range(0, step, LANES):
                folded[k] = folded[k] + values[:, lane:lane + LANES]
    for k, total in enumerate(folded):
        for part in range(step // LANES):
            row = k * (step // LANES) + part
            sums_ref[row:row + 1] = lane_sums(total[part * LANES:(part + 1) * LANES])


def load_blocks(refs):
    return [(ref, j * LANES) for ref in refs for j in range(ref.shape[1] // LANES)]


def row_kernel(z_ref, got_ref, *refs):
    blocks, out_ref = load_blocks(refs[:-1]), refs[-1]
    scale = 1.0 / (K * jnp.sum(got_ref[...], axis=0))
    totals = [jnp.zeros((SUB, LANES), jnp.float32) for _ in blocks]
    for b in range(scale.shape[0]):
        column = jnp.broadcast_to(scale[b:b + 1], (LANES, LANES)).T
        for j, (ref, lane) in enumerate(blocks):
            product = ref[b * LANES:(b + 1) * LANES, lane:lane + LANES] * column
            totals[j] = totals[j] + jnp.sum(product.reshape(LANES // SUB, SUB, LANES), axis=0)
    sums = [jnp.sum(total, axis=0, keepdims=True) for total in totals]
    group = len(sums) // 2
    own, other = jnp.concatenate(sums[:group], axis=0), jnp.concatenate(sums[group:], axis=0)
    first = z_ref[0] == 0
    tile = jnp.concatenate([jnp.where(first, own, other), jnp.where(first, other, own)], axis=0)
    for peer in range(out_ref.shape[0]):
        out_ref[peer] = tile


def row_scales(total_items, z_ref, got_ref):
    scale = 1.0 / (total_items * jnp.sum(got_ref[...], axis=0))
    group = scale.shape[0] // 2
    first = z_ref[0] == 0
    own, other = scale[:group], scale[group:]
    tiles = jnp.where(first, own, other), jnp.where(first, other, own)
    return [tile[row:row + 1] for tile in tiles for row in range(group)]


def col_kernel(total_items, z_ref, got_ref, *refs):
    blocks, out_ref = load_blocks(refs[:-1]), refs[-1]
    scales = row_scales(total_items, z_ref, got_ref)
    rows = []
    for b in range(out_ref.shape[1]):
        folded = jnp.zeros((LANES, LANES), jnp.float32)
        for (ref, lane), scale in zip(blocks, scales):
            folded = folded + ref[b * LANES:(b + 1) * LANES, lane:lane + LANES] * scale
        rows.append(lane_sums(folded))
    tile = jnp.concatenate(rows, axis=0)
    for peer in range(out_ref.shape[0]):
        out_ref[peer] = tile


def numer_kernel(total_items, count, z_ref, got_ref, *refs):
    high_refs, low_refs, out_ref = refs[count:2 * count], refs[2 * count:3 * count], refs[3 * count]
    scales = row_scales(total_items, z_ref, got_ref)
    codes, width = refs[0].shape[0], high_refs[0].shape[1]
    nx = out_ref.shape[0]
    parts = codes // LANES
    step = 256
    mass = []
    for start in range(0, codes, step):
        folded = jnp.zeros((step, LANES), jnp.float32)
        sums, at = None, 0
        for ref, xh_ref, xl_ref in zip(refs[:count], high_refs, low_refs):
            highs, lows = [], []
            for lane in range(0, ref.shape[1], LANES):
                weights = ref[start:start + step, lane:lane + LANES] * scales[at]
                folded = folded + weights
                high, low = split(weights)
                highs.append(high)
                lows.append(low)
                at += 1
            high, low = jnp.concatenate(highs, axis=1), jnp.concatenate(lows, axis=1)
            xh, xl = xh_ref[...], xl_ref[...]
            more = jnp.dot(high, xh, preferred_element_type=jnp.float32) + (
                jnp.dot(low, xh, preferred_element_type=jnp.float32)
                + jnp.dot(high, xl, preferred_element_type=jnp.float32)
            )
            sums = more if sums is None else sums + more
        for part in range(step // LANES):
            mass.append(lane_sums(folded[part * LANES:(part + 1) * LANES]))
            col = start // LANES + part
            for x in range(nx):
                for lane in range(x * width // nx, (x + 1) * width // nx, LANES):
                    turned = sums[part * LANES:(part + 1) * LANES, lane:lane + LANES].T
                    for group in range(LANES // SUB):
                        row = (lane - x * width // nx) // SUB + group
                        out_ref[x, row * parts + col] = turned[group * SUB:(group + 1) * SUB]
    tile = jnp.concatenate(mass + [jnp.ones((SUB - parts, LANES), jnp.float32)], axis=0)
    for x in range(nx):
        out_ref[x, out_ref.shape[1] - 1] = tile


def repack_kernel(got_ref, out_ref):
    summed = got_ref[0]
    for x in range(1, got_ref.shape[0]):
        summed = summed + got_ref[x]
    peers, count = out_ref.shape[0], out_ref.shape[1] - 1
    for peer in range(peers):
        out_ref[peer, :count] = summed[peer * count:(peer + 1) * count]
        out_ref[peer, count] = summed[peers * count]


def lookup_kernel(z_ref, index_ref, codes_ref, out_ref):
    part0 = codes_ref[...].astype(jnp.bfloat16)
    rest = codes_ref[...] - part0.astype(jnp.float32)
    part1 = rest.astype(jnp.bfloat16)
    part2 = (rest - part1.astype(jnp.float32)).astype(jnp.bfloat16)
    codes = codes_ref.shape[0]
    for block in range(out_ref.shape[0] // LANES):
        local = index_ref[block:block + 1] - z_ref[1]
        column = jnp.broadcast_to(local.astype(jnp.float32), (LANES, LANES)).T
        hits = []
        for b in range(codes // LANES):
            lane = lax.broadcasted_iota(jnp.int32, (LANES, LANES), 1) + b * LANES
            hits.append(jnp.where(column == lane.astype(jnp.float32), 1.0, 0.0).astype(jnp.bfloat16))
        chosen = jnp.concatenate(hits, axis=1)
        found = jnp.dot(chosen, part2, preferred_element_type=jnp.float32)
        found = jnp.dot(chosen, part1, preferred_element_type=jnp.float32) + found
        found = jnp.dot(chosen, part0, preferred_element_type=jnp.float32) + found
        out_ref[block * LANES:(block + 1) * LANES] = found


def finish_kernel(cores, got_ref, items_ref, looked_ref, out_ref, residual_ref):
    residual_ref[...] = items_ref[...] - looked_ref[...]
    peers, parts = got_ref.shape[0], got_ref.shape[1] - 1
    for core in range(cores):
        summed = got_ref[core]
        for peer in range(core + cores, peers, cores):
            summed = summed + got_ref[peer]
        for b in range(parts):
            lane = (core * parts + b) * LANES
            out_ref[:, lane:lane + LANES] = summed[b] / summed[parts][b:b + 1]


def body(items, codewords, assign):
    f32 = jnp.float32
    n = lax.axis_size("code")
    nx, ny, nc = lax.axis_size("x"), lax.axis_size("y"), lax.axis_size("core")
    local_codes, width = codewords.shape
    own_rows = items.shape[0]
    half = local_codes // nc
    total_items = own_rows * nc * n * nx * ny
    core = lax.axis_index("core")
    z_info = jnp.stack([core, lax.axis_index("code") * local_codes]).astype(jnp.int32)

    own = lax.all_gather(items, "code", axis=0, tiled=True)
    scaled = jax.ShapeDtypeStruct((half, width), jnp.bfloat16)
    code_high, code_low = call(scale_kernel, (scaled, scaled), [SMEM, VMEM])(z_info, codewords)
    index_tile = assign.reshape(-1, LANES)
    named = call(lookup_kernel, jax.ShapeDtypeStruct((assign.shape[0], width), f32), [SMEM, VMEM, VMEM], grant=12)(
        z_info, index_tile, codewords
    )
    own, named, code_high, code_low = lax.optimization_barrier((own, named, code_high, code_low))
    looked = lax.psum_scatter(named, "code", scatter_dimension=0, tiled=True)
    other = lax.ppermute(own, "core", [(0, 1), (1, 0)])

    def chunk(group):
        rows = group.shape[0]
        parts = jax.ShapeDtypeStruct((rows, width), jnp.bfloat16)
        shapes = (
            jax.ShapeDtypeStruct((half, rows), f32),
            jax.ShapeDtypeStruct((half // LANES, LANES), f32),
            parts,
            parts,
        )
        return call(chunk_kernel, shapes, [VMEM] * 3)(code_high, code_low, group)

    chunks = [chunk(own), chunk(other)]
    blocks = [c[0] for c in chunks]
    count = len(blocks)
    col_tile = chunks[0][1] + chunks[1][1]

    row_shape = jax.ShapeDtypeStruct((nc * n, nc * n, LANES), f32)
    col_shape = jax.ShapeDtypeStruct((nx * ny,) + col_tile.shape, f32)
    operands = [SMEM, VMEM] + [VMEM] * count
    cols = jnp.broadcast_to(col_tile[None], col_shape.shape)
    for turn in range(ITERS):
        got = lax.all_to_all(cols, ("x", "y"), 0, 0)
        rows = call(row_kernel, row_shape, operands)(z_info, got, *blocks)
        got = lax.all_to_all(rows, ("core", "code"), 0, 0)
        if turn < ITERS - 1:
            cols = call(functools.partial(col_kernel, total_items), col_shape, operands)(z_info, got, *blocks)

    per_owner = width // (nx * ny * nc)
    tiles = ny * nc * (per_owner // SUB) * (half // LANES)
    numer = call(
        functools.partial(numer_kernel, total_items, count),
        jax.ShapeDtypeStruct((nx, tiles + 1, SUB, LANES), f32),
        operands + [VMEM] * (2 * count),
        grant=16,
    )(z_info, got, *blocks, *[c[2] for c in chunks], *[c[3] for c in chunks])
    got = lax.all_to_all(numer, "x", 0, 0)
    got, looked = lax.optimization_barrier((got, looked))
    peers = ny * nc
    packed = call(repack_kernel, jax.ShapeDtypeStruct((peers, tiles // peers + 1, SUB, LANES), f32), [VMEM])(got)
    got = lax.all_to_all(packed, ("y", "core"), 0, 0)
    shapes = (jax.ShapeDtypeStruct((per_owner, local_codes), f32), jax.ShapeDtypeStruct(items.shape, f32))
    turned, residual = call(functools.partial(finish_kernel, nc), shapes, [VMEM] * 3)(got, items, looked)
    new_codewords = turned.T
    return (new_codewords, residual)


def solution(mesh):
    cores = 2
    ny = 8
    dp, code = mesh.devices.shape
    fine = Mesh(
        mesh.devices.reshape(dp // (ny * cores), ny, cores, code),
        ("x", "y", "core", "code"),
    )
    in_specs = (P(DP + ("code",), None), P("code", None), P(DP))
    out_specs = (P("code", DP), P(DP + ("code",), None))
    return jax.shard_map(body, mesh=fine, in_specs=in_specs, out_specs=out_specs, check_vma=False)
```

```python
import functools

import jax
import jax.numpy as jnp
from jax import lax
from jax.experimental import pallas as pl
from jax.experimental.pallas import tpu as pltpu
from jax.sharding import Mesh, PartitionSpec as P

K = 8192
ITERS = 3
DP = ("x", "y", "core")
LANES = 128
SUB = 8

epsilon = 1e-05
inverse_temp = 64.0

VMEM = pl.BlockSpec(memory_space=pltpu.VMEM)
SMEM = pl.BlockSpec(memory_space=pltpu.SMEM)
MIB = 1024 * 1024


def call(body, out_shape, ins, scratch=(), grant=8):
    return pl.pallas_call(
        body,
        out_shape=out_shape,
        in_specs=ins,
        out_specs=jax.tree.map(lambda _: VMEM, out_shape),
        scratch_shapes=list(scratch),
        compiler_params=pltpu.CompilerParams(vmem_limit_bytes=grant * MIB),
    )


def split(values):
    high = values.astype(jnp.bfloat16)
    return high, (values - high.astype(jnp.float32)).astype(jnp.bfloat16)


def unit_rows(values):
    return values * lax.rsqrt(jnp.mean(values * values, axis=-1, keepdims=True) + epsilon)


def dot_nt(a, b):
    return lax.dot_general(a, b, (((1,), (1,)), ((), ())), preferred_element_type=jnp.float32)


def lane_sums(block):
    return jnp.sum(block.T, axis=0, keepdims=True)


def scale_kernel(z_ref, codes_ref, high_ref, low_ref):
    half, width = high_ref.shape
    codes = codes_ref[pl.ds(pl.multiple_of(z_ref[0] * half, half), half)]
    high, low = split(unit_rows(codes) * (inverse_temp / width))
    high_ref[...] = high
    low_ref[...] = low


def chunk_kernel(high_ref, low_ref, items_ref, out_ref, sums_ref, xh_ref, xl_ref):
    codes, step = high_ref.shape[0], 256
    folded = [jnp.zeros((step, LANES), jnp.float32) for _ in range(0, codes, step)]
    for first in range(0, items_ref.shape[0], step):
        values = items_ref[first:first + step]
        xh_ref[first:first + step], xl_ref[first:first + step] = split(values)
        item_high, item_low = split(unit_rows(values))
        for k, start in enumerate(range(0, codes, step)):
            code_high = high_ref[start:start + step]
            code_low = low_ref[start:start + step]
            logits = dot_nt(code_high, item_high) + (dot_nt(code_high, item_low) + dot_nt(code_low, item_high))
            values = jnp.exp(logits)
            out_ref[start:start + step, first:first + step] = values
            for lane in range(0, step, LANES):
                folded[k] = folded[k] + values[:, lane:lane + LANES]
    rows = [lane_sums(total[at:at + LANES]) for total in folded for at in range(0, step, LANES)]

    @pl.when(pl.program_id(0) == 0)
    def _():
        sums_ref[...] = jnp.concatenate(rows, axis=0)

    @pl.when(pl.program_id(0) > 0)
    def _():
        sums_ref[...] += jnp.concatenate(rows, axis=0)


def load_blocks(refs):
    return [(ref, j * LANES) for ref in refs for j in range(ref.shape[1] // LANES)]


def row_kernel(got_ref, *refs):
    blocks, out_ref = load_blocks(refs[:-1]), refs[-1]
    scale = 1.0 / (K * jnp.sum(got_ref[...], axis=0))
    totals = [jnp.zeros((SUB, LANES), jnp.float32) for _ in blocks]
    for b in range(scale.shape[0]):
        column = jnp.broadcast_to(scale[b:b + 1], (LANES, LANES)).T
        for j, (ref, lane) in enumerate(blocks):
            product = ref[b * LANES:(b + 1) * LANES, lane:lane + LANES] * column
            totals[j] = totals[j] + jnp.sum(product.reshape(LANES // SUB, SUB, LANES), axis=0)
    sums = [jnp.sum(total, axis=0, keepdims=True) for total in totals]
    tile = jnp.concatenate(sums, axis=0)
    for peer in range(out_ref.shape[0]):
        out_ref[peer] = tile


def row_scales(total_items, got_ref):
    scale = 1.0 / (total_items * jnp.sum(got_ref[...], axis=0))
    return [scale[row:row + 1] for row in range(scale.shape[0])]


def col_kernel(total_items, got_ref, *refs):
    blocks, out_ref = load_blocks(refs[:-1]), refs[-1]
    scales = row_scales(total_items, got_ref)
    rows = []
    for b in range(out_ref.shape[1]):
        folded = jnp.zeros((LANES, LANES), jnp.float32)
        for (ref, lane), scale in zip(blocks, scales):
            folded = folded + ref[b * LANES:(b + 1) * LANES, lane:lane + LANES] * scale
        rows.append(lane_sums(folded))
    tile = jnp.concatenate(rows, axis=0)
    for peer in range(out_ref.shape[0]):
        out_ref[peer] = tile


def numer_kernel(total_items, count, got_ref, *refs):
    high_refs, low_refs, out_ref = refs[count:2 * count], refs[2 * count:3 * count], refs[3 * count]
    scales = row_scales(total_items, got_ref)
    codes, width = refs[0].shape[0], high_refs[0].shape[1]
    nx = out_ref.shape[0]
    parts = codes // LANES
    step = 256
    mass = []
    for start in range(0, codes, step):
        folded = jnp.zeros((step, LANES), jnp.float32)
        sums, at = None, 0
        for ref, xh_ref, xl_ref in zip(refs[:count], high_refs, low_refs):
            highs, lows = [], []
            for lane in range(0, ref.shape[1], LANES):
                weights = ref[start:start + step, lane:lane + LANES] * scales[at]
                folded = folded + weights
                high, low = split(weights)
                highs.append(high)
                lows.append(low)
                at += 1
            high, low = jnp.concatenate(highs, axis=1), jnp.concatenate(lows, axis=1)
            xh, xl = xh_ref[...], xl_ref[...]
            more = jnp.dot(high, xh, preferred_element_type=jnp.float32) + (
                jnp.dot(low, xh, preferred_element_type=jnp.float32)
                + jnp.dot(high, xl, preferred_element_type=jnp.float32)
            )
            sums = more if sums is None else sums + more
        for part in range(step // LANES):
            mass.append(lane_sums(folded[part * LANES:(part + 1) * LANES]))
            col = start // LANES + part
            for x in range(nx):
                for lane in range(x * width // nx, (x + 1) * width // nx, LANES):
                    turned = sums[part * LANES:(part + 1) * LANES, lane:lane + LANES].T
                    for group in range(LANES // SUB):
                        row = (lane - x * width // nx) // SUB + group
                        out_ref[x, row * parts + col] = turned[group * SUB:(group + 1) * SUB]
    tile = jnp.concatenate(mass + [jnp.ones((SUB - parts, LANES), jnp.float32)], axis=0)
    for x in range(nx):
        out_ref[x, out_ref.shape[1] - 1] = tile


def repack_kernel(got_ref, out_ref):
    summed = got_ref[0]
    for x in range(1, got_ref.shape[0]):
        summed = summed + got_ref[x]
    peers, count = out_ref.shape[0], out_ref.shape[1] - 1
    for peer in range(peers):
        out_ref[peer, :count] = summed[peer * count:(peer + 1) * count]
        out_ref[peer, count] = summed[peers * count]


def lookup_kernel(z_ref, index_ref, codes_ref, out_ref):
    part0 = codes_ref[...].astype(jnp.bfloat16)
    rest = codes_ref[...] - part0.astype(jnp.float32)
    part1 = rest.astype(jnp.bfloat16)
    part2 = (rest - part1.astype(jnp.float32)).astype(jnp.bfloat16)
    codes = codes_ref.shape[0]
    for block in range(out_ref.shape[0] // LANES):
        local = index_ref[block:block + 1] - z_ref[1]
        column = jnp.broadcast_to(local.astype(jnp.float32), (LANES, LANES)).T
        hits = []
        for b in range(codes // LANES):
            lane = lax.broadcasted_iota(jnp.int32, (LANES, LANES), 1) + b * LANES
            hits.append(jnp.where(column == lane.astype(jnp.float32), 1.0, 0.0).astype(jnp.bfloat16))
        chosen = jnp.concatenate(hits, axis=1)
        found = jnp.dot(chosen, part2, preferred_element_type=jnp.float32)
        found = jnp.dot(chosen, part1, preferred_element_type=jnp.float32) + found
        found = jnp.dot(chosen, part0, preferred_element_type=jnp.float32) + found
        out_ref[block * LANES:(block + 1) * LANES] = found


def finish_kernel(cores, got_ref, items_ref, looked_ref, out_ref, residual_ref):
    residual_ref[...] = items_ref[...] - looked_ref[...]
    peers, parts = got_ref.shape[0], got_ref.shape[1] - 1
    for core in range(cores):
        summed = got_ref[core]
        for peer in range(core + cores, peers, cores):
            summed = summed + got_ref[peer]
        for b in range(parts):
            lane = (core * parts + b) * LANES
            out_ref[:, lane:lane + LANES] = summed[b] / summed[parts][b:b + 1]


def body(items, codewords, assign):
    f32 = jnp.float32
    n = lax.axis_size("code")
    nx, ny, nc = lax.axis_size("x"), lax.axis_size("y"), lax.axis_size("core")
    local_codes, width = codewords.shape
    own_rows = items.shape[0]
    half = local_codes // nc
    total_items = own_rows * nc * n * nx * ny
    core = lax.axis_index("core")
    z_info = jnp.stack([core, lax.axis_index("code") * local_codes]).astype(jnp.int32)

    gathered = lax.all_gather(items, ("core", "code"), axis=0, tiled=True)
    scaled = jax.ShapeDtypeStruct((half, width), jnp.bfloat16)
    code_high, code_low = call(scale_kernel, (scaled, scaled), [SMEM, VMEM])(z_info, codewords)
    index_tile = assign.reshape(-1, LANES)
    named = call(lookup_kernel, jax.ShapeDtypeStruct((assign.shape[0], width), f32), [SMEM, VMEM, VMEM], grant=12)(
        z_info, index_tile, codewords
    )
    gathered, named, code_high, code_low = lax.optimization_barrier((gathered, named, code_high, code_low))
    looked = lax.psum_scatter(named, "code", scatter_dimension=0, tiled=True)
    group, block = gathered.shape[0], 256
    part = jax.ShapeDtypeStruct((group, width), jnp.bfloat16)
    kernel_vals, col_tile, item_high, item_low = pl.pallas_call(
        chunk_kernel,
        grid=(group // block,),
        out_shape=(
            jax.ShapeDtypeStruct((half, group), f32),
            jax.ShapeDtypeStruct((half // LANES, LANES), f32),
            part,
            part,
        ),
        in_specs=[
            pl.BlockSpec((half, width), lambda i: (0, 0)),
            pl.BlockSpec((half, width), lambda i: (0, 0)),
            pl.BlockSpec((block, width), lambda i: (i, 0)),
        ],
        out_specs=(
            pl.BlockSpec((half, block), lambda i: (0, i)),
            pl.BlockSpec((half // LANES, LANES), lambda i: (0, 0)),
            pl.BlockSpec((block, width), lambda i: (i, 0)),
            pl.BlockSpec((block, width), lambda i: (i, 0)),
        ),
        compiler_params=pltpu.CompilerParams(vmem_limit_bytes=16 * MIB),
    )(code_high, code_low, pltpu.with_memory_space_constraint(gathered, pltpu.HBM))
    blocks, count = [kernel_vals], 1

    row_shape = jax.ShapeDtypeStruct((nc * n, nc * n, LANES), f32)
    col_shape = jax.ShapeDtypeStruct((nx * ny,) + col_tile.shape, f32)
    operands = [VMEM] * (1 + count)
    cols = jnp.broadcast_to(col_tile[None], col_shape.shape)
    for turn in range(ITERS):
        got = lax.all_to_all(cols, ("x", "y"), 0, 0)
        rows = call(row_kernel, row_shape, operands)(got, *blocks)
        got = lax.all_to_all(rows, ("core", "code"), 0, 0)
        if turn < ITERS - 1:
            cols = call(functools.partial(col_kernel, total_items), col_shape, operands)(got, *blocks)

    per_owner = width // (nx * ny * nc)
    tiles = ny * nc * (per_owner // SUB) * (half // LANES)
    numer = call(
        functools.partial(numer_kernel, total_items, count),
        jax.ShapeDtypeStruct((nx, tiles + 1, SUB, LANES), f32),
        operands + [VMEM] * (2 * count),
        grant=16,
    )(got, *blocks, item_high, item_low)
    got = lax.all_to_all(numer, "x", 0, 0)
    got, looked = lax.optimization_barrier((got, looked))
    peers = ny * nc
    packed = call(repack_kernel, jax.ShapeDtypeStruct((peers, tiles // peers + 1, SUB, LANES), f32), [VMEM])(got)
    got = lax.all_to_all(packed, ("y", "core"), 0, 0)
    shapes = (jax.ShapeDtypeStruct((per_owner, local_codes), f32), jax.ShapeDtypeStruct(items.shape, f32))
    turned, residual = call(functools.partial(finish_kernel, nc), shapes, [VMEM] * 3)(got, items, looked)
    new_codewords = turned.T
    return (new_codewords, residual)


def solution(mesh):
    cores = 2
    ny = 8
    dp, code = mesh.devices.shape
    fine = Mesh(
        mesh.devices.reshape(dp // (ny * cores), ny, cores, code),
        ("x", "y", "core", "code"),
    )
    in_specs = (P(DP + ("code",), None), P("code", None), P(DP))
    out_specs = (P("code", DP), P(DP + ("code",), None))
    return jax.shard_map(body, mesh=fine, in_specs=in_specs, out_specs=out_specs, check_vma=False)
```

```python
import functools

import jax
import jax.numpy as jnp
from jax import lax
from jax.experimental import pallas as pl
from jax.experimental.pallas import tpu as pltpu
from jax.sharding import Mesh, PartitionSpec as P

K = 8192
ITERS = 3
DP = ("x", "yh", "yl", "core")
LANES = 128
SUB = 8

epsilon = 1e-05
inverse_temp = 64.0

VMEM = pl.BlockSpec(memory_space=pltpu.VMEM)
SMEM = pl.BlockSpec(memory_space=pltpu.SMEM)
MIB = 1024 * 1024


def call(body, out_shape, ins, scratch=(), grant=8):
    return pl.pallas_call(
        body,
        out_shape=out_shape,
        in_specs=ins,
        out_specs=jax.tree.map(lambda _: VMEM, out_shape),
        scratch_shapes=list(scratch),
        compiler_params=pltpu.CompilerParams(vmem_limit_bytes=grant * MIB),
    )


def split(values):
    high = values.astype(jnp.bfloat16)
    return high, (values - high.astype(jnp.float32)).astype(jnp.bfloat16)


def unit_rows(values):
    return values * lax.rsqrt(jnp.mean(values * values, axis=-1, keepdims=True) + epsilon)


def dot_nt(a, b):
    return lax.dot_general(a, b, (((1,), (1,)), ((), ())), preferred_element_type=jnp.float32)


def lane_sums(block):
    return jnp.sum(block.T, axis=0, keepdims=True)


def scale_kernel(z_ref, codes_ref, high_ref, low_ref):
    half, width = high_ref.shape
    codes = codes_ref[pl.ds(pl.multiple_of(z_ref[0] * half, half), half)]
    high, low = split(unit_rows(codes) * (inverse_temp / width))
    high_ref[...] = high
    low_ref[...] = low


def chunk_kernel(high_ref, low_ref, items_ref, out_ref, sums_ref, xh_ref, xl_ref, held_ref, sems):
    codes, step = high_ref.shape[0], 256
    starts = range(0, items_ref.shape[0], step)
    copies = [
        pltpu.make_async_copy(items_ref.at[pl.ds(first, step)], held_ref.at[pl.ds(first, step)], sems.at[i])
        for i, first in enumerate(starts)
    ]
    for copy in copies:
        copy.start()
    folded = [jnp.zeros((step, LANES), jnp.float32) for _ in range(0, codes, step)]
    for copy, first in zip(copies, starts):
        copy.wait()
        values = held_ref[first:first + step]
        xh_ref[first:first + step], xl_ref[first:first + step] = split(values)
        item_high, item_low = split(unit_rows(values))
        for k, start in enumerate(range(0, codes, step)):
            code_high = high_ref[start:start + step]
            code_low = low_ref[start:start + step]
            logits = dot_nt(code_high, item_high) + (dot_nt(code_high, item_low) + dot_nt(code_low, item_high))
            values = jnp.exp(logits)
            out_ref[start:start + step, first:first + step] = values
            for lane in range(0, step, LANES):
                folded[k] = folded[k] + values[:, lane:lane + LANES]
    for k, total in enumerate(folded):
        for part in range(step // LANES):
            row = k * (step // LANES) + part
            sums_ref[row:row + 1] = lane_sums(total[part * LANES:(part + 1) * LANES])


def load_blocks(refs):
    return [(ref, j * LANES) for ref in refs for j in range(ref.shape[1] // LANES)]


def row_kernel(got_ref, *refs):
    blocks, out_ref = load_blocks(refs[:-1]), refs[-1]
    scale = 1.0 / (K * jnp.sum(got_ref[...], axis=0))
    totals = [jnp.zeros((SUB, LANES), jnp.float32) for _ in blocks]
    for b in range(scale.shape[0]):
        column = jnp.broadcast_to(scale[b:b + 1], (LANES, LANES)).T
        for j, (ref, lane) in enumerate(blocks):
            product = ref[b * LANES:(b + 1) * LANES, lane:lane + LANES] * column
            totals[j] = totals[j] + jnp.sum(product.reshape(LANES // SUB, SUB, LANES), axis=0)
    sums = [jnp.sum(total, axis=0, keepdims=True) for total in totals]
    tile = jnp.concatenate(sums, axis=0)
    for peer in range(out_ref.shape[0]):
        out_ref[peer] = tile


def row_scales(total_items, got_ref):
    scale = 1.0 / (total_items * jnp.sum(got_ref[...], axis=0))
    return [scale[row:row + 1] for row in range(scale.shape[0])]


def col_kernel(total_items, got_ref, *refs):
    blocks, out_ref = load_blocks(refs[:-1]), refs[-1]
    scales = row_scales(total_items, got_ref)
    rows = []
    for b in range(out_ref.shape[1]):
        folded = jnp.zeros((LANES, LANES), jnp.float32)
        for (ref, lane), scale in zip(blocks, scales):
            folded = folded + ref[b * LANES:(b + 1) * LANES, lane:lane + LANES] * scale
        rows.append(lane_sums(folded))
    tile = jnp.concatenate(rows, axis=0)
    for peer in range(out_ref.shape[0]):
        out_ref[peer] = tile


def numer_kernel(total_items, count, nx, near, cores, got_ref, *refs):
    high_refs, low_refs, out_ref = refs[count:2 * count], refs[2 * count:3 * count], refs[3 * count]
    scales = row_scales(total_items, got_ref)
    codes, width = refs[0].shape[0], high_refs[0].shape[1]
    parts = codes // LANES
    per_x = width // (nx * SUB)
    step = 256
    mass = []
    for start in range(0, codes, step):
        folded = jnp.zeros((step, LANES), jnp.float32)
        sums, at = None, 0
        for ref, xh_ref, xl_ref in zip(refs[:count], high_refs, low_refs):
            highs, lows = [], []
            for lane in range(0, ref.shape[1], LANES):
                weights = ref[start:start + step, lane:lane + LANES] * scales[at]
                folded = folded + weights
                high, low = split(weights)
                highs.append(high)
                lows.append(low)
                at += 1
            high, low = jnp.concatenate(highs, axis=1), jnp.concatenate(lows, axis=1)
            xh, xl = xh_ref[...], xl_ref[...]
            more = jnp.dot(high, xh, preferred_element_type=jnp.float32) + (
                jnp.dot(low, xh, preferred_element_type=jnp.float32)
                + jnp.dot(high, xl, preferred_element_type=jnp.float32)
            )
            sums = more if sums is None else sums + more
        for part in range(step // LANES):
            mass.append(lane_sums(folded[part * LANES:(part + 1) * LANES]))
            col = start // LANES + part
            for lane in range(0, width, LANES):
                turned = sums[part * LANES:(part + 1) * LANES, lane:lane + LANES].T
                for group in range(LANES // SUB):
                    x, rest = divmod(lane // SUB + group, per_x)
                    y, core = divmod(rest, cores)
                    row = (y // near) * cores + core
                    out_ref[x * near + y % near, row * parts + col] = turned[group * SUB:(group + 1) * SUB]
    tile = jnp.concatenate(mass + [jnp.ones((SUB - parts, LANES), jnp.float32)], axis=0)
    for peer in range(out_ref.shape[0]):
        out_ref[peer, out_ref.shape[1] - 1] = tile


def repack_kernel(got_ref, out_ref):
    summed = got_ref[0]
    for x in range(1, got_ref.shape[0]):
        summed = summed + got_ref[x]
    peers, count = out_ref.shape[0], out_ref.shape[1] - 1
    for peer in range(peers):
        out_ref[peer, :count] = summed[peer * count:(peer + 1) * count]
        out_ref[peer, count] = summed[peers * count]


def lookup_kernel(z_ref, index_ref, codes_ref, out_ref):
    part0 = codes_ref[...].astype(jnp.bfloat16)
    rest = codes_ref[...] - part0.astype(jnp.float32)
    part1 = rest.astype(jnp.bfloat16)
    part2 = (rest - part1.astype(jnp.float32)).astype(jnp.bfloat16)
    codes = codes_ref.shape[0]
    for block in range(out_ref.shape[0] // LANES):
        local = index_ref[block:block + 1] - z_ref[1]
        column = jnp.broadcast_to(local.astype(jnp.float32), (LANES, LANES)).T
        hits = []
        for b in range(codes // LANES):
            lane = lax.broadcasted_iota(jnp.int32, (LANES, LANES), 1) + b * LANES
            hits.append(jnp.where(column == lane.astype(jnp.float32), 1.0, 0.0).astype(jnp.bfloat16))
        chosen = jnp.concatenate(hits, axis=1)
        found = jnp.dot(chosen, part2, preferred_element_type=jnp.float32)
        found = jnp.dot(chosen, part1, preferred_element_type=jnp.float32) + found
        found = jnp.dot(chosen, part0, preferred_element_type=jnp.float32) + found
        out_ref[block * LANES:(block + 1) * LANES] = found


def finish_kernel(cores, got_ref, items_ref, looked_ref, out_ref, residual_ref):
    residual_ref[...] = items_ref[...] - looked_ref[...]
    peers, parts = got_ref.shape[0], got_ref.shape[1] - 1
    for core in range(cores):
        summed = got_ref[core]
        for peer in range(core + cores, peers, cores):
            summed = summed + got_ref[peer]
        for b in range(parts):
            lane = (core * parts + b) * LANES
            out_ref[:, lane:lane + LANES] = summed[b] / summed[parts][b:b + 1]


def body(items, codewords, assign):
    f32 = jnp.float32
    n = lax.axis_size("code")
    nx, nc = lax.axis_size("x"), lax.axis_size("core")
    high, low = lax.axis_size("yh"), lax.axis_size("yl")
    ny = high * low
    local_codes, width = codewords.shape
    own_rows = items.shape[0]
    half = local_codes // nc
    total_items = own_rows * nc * n * nx * ny
    core = lax.axis_index("core")
    z_info = jnp.stack([core, lax.axis_index("code") * local_codes]).astype(jnp.int32)

    gathered = lax.all_gather(items, ("core", "code"), axis=0, tiled=True)
    scaled = jax.ShapeDtypeStruct((half, width), jnp.bfloat16)
    code_high, code_low = call(scale_kernel, (scaled, scaled), [SMEM, VMEM])(z_info, codewords)
    index_tile = assign.reshape(-1, LANES)
    named = call(lookup_kernel, jax.ShapeDtypeStruct((assign.shape[0], width), f32), [SMEM, VMEM, VMEM], grant=12)(
        z_info, index_tile, codewords
    )
    gathered, named, code_high, code_low = lax.optimization_barrier((gathered, named, code_high, code_low))
    looked = lax.psum_scatter(named, "code", scatter_dimension=0, tiled=True)
    group = gathered.shape[0]
    part = jax.ShapeDtypeStruct((group, width), jnp.bfloat16)
    kernel_vals, col_tile, item_high, item_low = call(
        chunk_kernel,
        (
            jax.ShapeDtypeStruct((half, group), f32),
            jax.ShapeDtypeStruct((half // LANES, LANES), f32),
            part,
            part,
        ),
        [VMEM, VMEM, pl.BlockSpec(memory_space=pl.ANY)],
        [pltpu.VMEM((group, width), f32), pltpu.SemaphoreType.DMA((group // 256,))],
        grant=16,
    )(code_high, code_low, pltpu.with_memory_space_constraint(gathered, pltpu.HBM))
    blocks, count = [kernel_vals], 1

    row_shape = jax.ShapeDtypeStruct((nc * n, nc * n, LANES), f32)
    col_shape = jax.ShapeDtypeStruct((nx * ny,) + col_tile.shape, f32)
    operands = [VMEM] * (1 + count)
    cols = jnp.broadcast_to(col_tile[None], col_shape.shape)
    for turn in range(ITERS):
        got = lax.all_to_all(cols, ("x", "yh", "yl"), 0, 0)
        rows = call(row_kernel, row_shape, operands)(got, *blocks)
        got = lax.all_to_all(rows, ("core", "code"), 0, 0)
        if turn < ITERS - 1:
            cols = call(functools.partial(col_kernel, total_items), col_shape, operands)(got, *blocks)

    per_owner = width // (nx * ny * nc)
    tiles = high * nc * (per_owner // SUB) * (half // LANES)
    numer = call(
        functools.partial(numer_kernel, total_items, count, nx, low, nc),
        jax.ShapeDtypeStruct((nx * low, tiles + 1, SUB, LANES), f32),
        operands + [VMEM] * (2 * count),
        grant=16,
    )(got, *blocks, item_high, item_low)
    got = lax.all_to_all(numer, ("x", "yl"), 0, 0)
    got, looked = lax.optimization_barrier((got, looked))
    peers = high * nc
    packed = call(repack_kernel, jax.ShapeDtypeStruct((peers, tiles // peers + 1, SUB, LANES), f32), [VMEM])(got)
    got = lax.all_to_all(packed, ("yh", "core"), 0, 0)
    shapes = (jax.ShapeDtypeStruct((per_owner, local_codes), f32), jax.ShapeDtypeStruct(items.shape, f32))
    turned, residual = call(functools.partial(finish_kernel, nc), shapes, [VMEM] * 3)(got, items, looked)
    new_codewords = turned.T
    return (new_codewords, residual)


def solution(mesh):
    cores = 2
    high, low = 4, 2
    dp, code = mesh.devices.shape
    fine = Mesh(
        mesh.devices.reshape(dp // (high * low * cores), high, low, cores, code),
        ("x", "yh", "yl", "core", "code"),
    )
    in_specs = (P(DP + ("code",), None), P("code", None), P(DP))
    out_specs = (P("code", DP), P(DP + ("code",), None))
    return jax.shard_map(body, mesh=fine, in_specs=in_specs, out_specs=out_specs, check_vma=False)
```

```python
import functools

import jax
import jax.numpy as jnp
from jax import lax
from jax.experimental import pallas as pl
from jax.experimental.pallas import tpu as pltpu
from jax.sharding import Mesh, PartitionSpec as P

K = 8192
ITERS = 3
DP = ("x", "yh", "yl", "core")
LANES = 128
SUB = 8

epsilon = 1e-05
inverse_temp = 64.0

VMEM = pl.BlockSpec(memory_space=pltpu.VMEM)
SMEM = pl.BlockSpec(memory_space=pltpu.SMEM)
MIB = 1024 * 1024


def call(body, out_shape, ins, scratch=(), grant=8):
    return pl.pallas_call(
        body,
        out_shape=out_shape,
        in_specs=ins,
        out_specs=jax.tree.map(lambda _: VMEM, out_shape),
        scratch_shapes=list(scratch),
        compiler_params=pltpu.CompilerParams(vmem_limit_bytes=grant * MIB),
    )


def split(values):
    high = values.astype(jnp.bfloat16)
    return high, (values - high.astype(jnp.float32)).astype(jnp.bfloat16)


def unit_rows(values):
    return values * lax.rsqrt(jnp.mean(values * values, axis=-1, keepdims=True) + epsilon)


def dot_nt(a, b):
    return lax.dot_general(a, b, (((1,), (1,)), ((), ())), preferred_element_type=jnp.float32)


def lane_sums(block):
    return jnp.sum(block.T, axis=0, keepdims=True)


def scale_kernel(z_ref, codes_ref, high_ref, low_ref):
    half, width = high_ref.shape
    codes = codes_ref[pl.ds(pl.multiple_of(z_ref[0] * half, half), half)]
    high, low = split(unit_rows(codes) * (inverse_temp / width))
    high_ref[...] = high
    low_ref[...] = low


def chunk_kernel(high_ref, low_ref, items_ref, out_ref, sums_ref, xh_ref, xl_ref, held_ref, sems):
    codes, step = high_ref.shape[0], 256
    total = items_ref.shape[0]
    edges = [0, step, total // 2, total]
    copies = [
        pltpu.make_async_copy(items_ref.at[pl.ds(a, b - a)], held_ref.at[pl.ds(a, b - a)], sems.at[i])
        for i, (a, b) in enumerate(zip(edges, edges[1:]))
    ]
    for copy in copies:
        copy.start()
    folded = [jnp.zeros((step, LANES), jnp.float32) for _ in range(0, codes, step)]
    for copy, begin, end in zip(copies, edges, edges[1:]):
        copy.wait()
        for first in range(begin, end, step):
            values = held_ref[first:first + step]
            xh_ref[first:first + step], xl_ref[first:first + step] = split(values)
            item_high, item_low = split(unit_rows(values))
            for k, start in enumerate(range(0, codes, step)):
                code_high = high_ref[start:start + step]
                code_low = low_ref[start:start + step]
                logits = dot_nt(code_high, item_high) + (dot_nt(code_high, item_low) + dot_nt(code_low, item_high))
                values = jnp.exp(logits)
                out_ref[start:start + step, first:first + step] = values
                for lane in range(0, step, LANES):
                    folded[k] = folded[k] + values[:, lane:lane + LANES]
    for k, total in enumerate(folded):
        for part in range(step // LANES):
            row = k * (step // LANES) + part
            sums_ref[row:row + 1] = lane_sums(total[part * LANES:(part + 1) * LANES])


def load_blocks(refs):
    return [(ref, j * LANES) for ref in refs for j in range(ref.shape[1] // LANES)]


def row_kernel(got_ref, *refs):
    blocks, out_ref = load_blocks(refs[:-1]), refs[-1]
    scale = 1.0 / (K * jnp.sum(got_ref[...], axis=0))
    totals = [jnp.zeros((SUB, LANES), jnp.float32) for _ in blocks]
    for b in range(scale.shape[0]):
        column = jnp.broadcast_to(scale[b:b + 1], (LANES, LANES)).T
        for j, (ref, lane) in enumerate(blocks):
            product = ref[b * LANES:(b + 1) * LANES, lane:lane + LANES] * column
            totals[j] = totals[j] + jnp.sum(product.reshape(LANES // SUB, SUB, LANES), axis=0)
    sums = [jnp.sum(total, axis=0, keepdims=True) for total in totals]
    tile = jnp.concatenate(sums, axis=0)
    for peer in range(out_ref.shape[0]):
        out_ref[peer] = tile


def row_scales(total_items, got_ref):
    scale = 1.0 / (total_items * jnp.sum(got_ref[...], axis=0))
    return [scale[row:row + 1] for row in range(scale.shape[0])]


def col_kernel(total_items, got_ref, *refs):
    blocks, out_ref = load_blocks(refs[:-1]), refs[-1]
    scales = row_scales(total_items, got_ref)
    rows = []
    for b in range(out_ref.shape[1]):
        folded = jnp.zeros((LANES, LANES), jnp.float32)
        for (ref, lane), scale in zip(blocks, scales):
            folded = folded + ref[b * LANES:(b + 1) * LANES, lane:lane + LANES] * scale
        rows.append(lane_sums(folded))
    tile = jnp.concatenate(rows, axis=0)
    for peer in range(out_ref.shape[0]):
        out_ref[peer] = tile


def numer_kernel(total_items, count, nx, near, cores, got_ref, *refs):
    high_refs, low_refs, out_ref = refs[count:2 * count], refs[2 * count:3 * count], refs[3 * count]
    scales = row_scales(total_items, got_ref)
    codes, width = refs[0].shape[0], high_refs[0].shape[1]
    parts = codes // LANES
    per_x = width // (nx * SUB)
    step = 256
    mass = []
    for start in range(0, codes, step):
        folded = jnp.zeros((step, LANES), jnp.float32)
        sums, at = None, 0
        for ref, xh_ref, xl_ref in zip(refs[:count], high_refs, low_refs):
            highs, lows = [], []
            for lane in range(0, ref.shape[1], LANES):
                weights = ref[start:start + step, lane:lane + LANES] * scales[at]
                folded = folded + weights
                high, low = split(weights)
                highs.append(high)
                lows.append(low)
                at += 1
            high, low = jnp.concatenate(highs, axis=1), jnp.concatenate(lows, axis=1)
            xh, xl = xh_ref[...], xl_ref[...]
            more = jnp.dot(high, xh, preferred_element_type=jnp.float32) + (
                jnp.dot(low, xh, preferred_element_type=jnp.float32)
                + jnp.dot(high, xl, preferred_element_type=jnp.float32)
            )
            sums = more if sums is None else sums + more
        for part in range(step // LANES):
            mass.append(lane_sums(folded[part * LANES:(part + 1) * LANES]))
            col = start // LANES + part
            for lane in range(0, width, LANES):
                turned = sums[part * LANES:(part + 1) * LANES, lane:lane + LANES].T
                for group in range(LANES // SUB):
                    x, rest = divmod(lane // SUB + group, per_x)
                    y, core = divmod(rest, cores)
                    row = (y // near) * cores + core
                    out_ref[x * near + y % near, row * parts + col] = turned[group * SUB:(group + 1) * SUB]
    tile = jnp.concatenate(mass + [jnp.ones((SUB - parts, LANES), jnp.float32)], axis=0)
    for peer in range(out_ref.shape[0]):
        out_ref[peer, out_ref.shape[1] - 1] = tile


def repack_kernel(got_ref, out_ref):
    summed = got_ref[0]
    for x in range(1, got_ref.shape[0]):
        summed = summed + got_ref[x]
    peers, count = out_ref.shape[0], out_ref.shape[1] - 1
    for peer in range(peers):
        out_ref[peer, :count] = summed[peer * count:(peer + 1) * count]
        out_ref[peer, count] = summed[peers * count]


def lookup_kernel(z_ref, index_ref, codes_ref, out_ref):
    part0 = codes_ref[...].astype(jnp.bfloat16)
    rest = codes_ref[...] - part0.astype(jnp.float32)
    part1 = rest.astype(jnp.bfloat16)
    part2 = (rest - part1.astype(jnp.float32)).astype(jnp.bfloat16)
    codes = codes_ref.shape[0]
    for block in range(out_ref.shape[0] // LANES):
        local = index_ref[block:block + 1] - z_ref[1]
        column = jnp.broadcast_to(local.astype(jnp.float32), (LANES, LANES)).T
        hits = []
        for b in range(codes // LANES):
            lane = lax.broadcasted_iota(jnp.int32, (LANES, LANES), 1) + b * LANES
            hits.append(jnp.where(column == lane.astype(jnp.float32), 1.0, 0.0).astype(jnp.bfloat16))
        chosen = jnp.concatenate(hits, axis=1)
        found = jnp.dot(chosen, part2, preferred_element_type=jnp.float32)
        found = jnp.dot(chosen, part1, preferred_element_type=jnp.float32) + found
        found = jnp.dot(chosen, part0, preferred_element_type=jnp.float32) + found
        out_ref[block * LANES:(block + 1) * LANES] = found


def finish_kernel(cores, got_ref, items_ref, looked_ref, out_ref, residual_ref):
    residual_ref[...] = items_ref[...] - looked_ref[...]
    peers, parts = got_ref.shape[0], got_ref.shape[1] - 1
    for core in range(cores):
        summed = got_ref[core]
        for peer in range(core + cores, peers, cores):
            summed = summed + got_ref[peer]
        for b in range(parts):
            lane = (core * parts + b) * LANES
            out_ref[:, lane:lane + LANES] = summed[b] / summed[parts][b:b + 1]


def body(items, codewords, assign):
    f32 = jnp.float32
    n = lax.axis_size("code")
    nx, nc = lax.axis_size("x"), lax.axis_size("core")
    high, low = lax.axis_size("yh"), lax.axis_size("yl")
    ny = high * low
    local_codes, width = codewords.shape
    own_rows = items.shape[0]
    half = local_codes // nc
    total_items = own_rows * nc * n * nx * ny
    core = lax.axis_index("core")
    z_info = jnp.stack([core, lax.axis_index("code") * local_codes]).astype(jnp.int32)

    gathered = lax.all_gather(items, ("core", "code"), axis=0, tiled=True)
    scaled = jax.ShapeDtypeStruct((half, width), jnp.bfloat16)
    code_high, code_low = call(scale_kernel, (scaled, scaled), [SMEM, VMEM])(z_info, codewords)
    index_tile = assign.reshape(-1, LANES)
    named = call(lookup_kernel, jax.ShapeDtypeStruct((assign.shape[0], width), f32), [SMEM, VMEM, VMEM], grant=12)(
        z_info, index_tile, codewords
    )
    gathered, named, code_high, code_low = lax.optimization_barrier((gathered, named, code_high, code_low))
    looked = lax.psum_scatter(named, "code", scatter_dimension=0, tiled=True)
    group = gathered.shape[0]
    part = jax.ShapeDtypeStruct((group, width), jnp.bfloat16)
    kernel_vals, col_tile, item_high, item_low = call(
        chunk_kernel,
        (
            jax.ShapeDtypeStruct((half, group), f32),
            jax.ShapeDtypeStruct((half // LANES, LANES), f32),
            part,
            part,
        ),
        [VMEM, VMEM, pl.BlockSpec(memory_space=pl.ANY)],
        [pltpu.VMEM((group, width), f32), pltpu.SemaphoreType.DMA((3,))],
        grant=16,
    )(code_high, code_low, pltpu.with_memory_space_constraint(gathered, pltpu.HBM))
    blocks, count = [kernel_vals], 1

    row_shape = jax.ShapeDtypeStruct((nc * n, nc * n, LANES), f32)
    col_shape = jax.ShapeDtypeStruct((nx * ny,) + col_tile.shape, f32)
    operands = [VMEM] * (1 + count)
    cols = jnp.broadcast_to(col_tile[None], col_shape.shape)
    for turn in range(ITERS):
        got = lax.all_to_all(cols, ("x", "yh", "yl"), 0, 0)
        rows = call(row_kernel, row_shape, operands)(got, *blocks)
        got = lax.all_to_all(rows, ("core", "code"), 0, 0)
        if turn < ITERS - 1:
            cols = call(functools.partial(col_kernel, total_items), col_shape, operands)(got, *blocks)

    per_owner = width // (nx * ny * nc)
    tiles = high * nc * (per_owner // SUB) * (half // LANES)
    numer = call(
        functools.partial(numer_kernel, total_items, count, nx, low, nc),
        jax.ShapeDtypeStruct((nx * low, tiles + 1, SUB, LANES), f32),
        operands + [VMEM] * (2 * count),
        grant=16,
    )(got, *blocks, item_high, item_low)
    numer, looked = lax.optimization_barrier((numer, looked))
    got = lax.all_to_all(numer, ("x", "yl"), 0, 0)
    peers = high * nc
    packed = call(repack_kernel, jax.ShapeDtypeStruct((peers, tiles // peers + 1, SUB, LANES), f32), [VMEM])(got)
    got = lax.all_to_all(packed, ("yh", "core"), 0, 0)
    shapes = (jax.ShapeDtypeStruct((per_owner, local_codes), f32), jax.ShapeDtypeStruct(items.shape, f32))
    turned, residual = call(functools.partial(finish_kernel, nc), shapes, [VMEM] * 3)(got, items, looked)
    new_codewords = turned.T
    return (new_codewords, residual)


def solution(mesh):
    cores = 2
    high, low = 4, 2
    dp, code = mesh.devices.shape
    fine = Mesh(
        mesh.devices.reshape(dp // (high * low * cores), high, low, cores, code),
        ("x", "yh", "yl", "core", "code"),
    )
    in_specs = (P(DP + ("code",), None), P("code", None), P(DP))
    out_specs = (P("code", DP), P(DP + ("code",), None))
    return jax.shard_map(body, mesh=fine, in_specs=in_specs, out_specs=out_specs, check_vma=False)
```

```python
import functools

import jax
import jax.numpy as jnp
from jax import lax
from jax.experimental import pallas as pl
from jax.experimental.pallas import tpu as pltpu
from jax.sharding import Mesh, PartitionSpec as P

K = 8192
ITERS = 3
DP = ("x", "yh", "yl", "core")
LANES = 128
SUB = 8

epsilon = 1e-05
inverse_temp = 64.0

VMEM = pl.BlockSpec(memory_space=pltpu.VMEM)
SMEM = pl.BlockSpec(memory_space=pltpu.SMEM)
MIB = 1024 * 1024


def call(body, out_shape, ins, scratch=(), grant=8):
    return pl.pallas_call(
        body,
        out_shape=out_shape,
        in_specs=ins,
        out_specs=jax.tree.map(lambda _: VMEM, out_shape),
        scratch_shapes=list(scratch),
        compiler_params=pltpu.CompilerParams(vmem_limit_bytes=grant * MIB),
    )


def split(values):
    high = values.astype(jnp.bfloat16)
    return high, (values - high.astype(jnp.float32)).astype(jnp.bfloat16)


def unit_rows(values):
    return values * lax.rsqrt(jnp.mean(values * values, axis=-1, keepdims=True) + epsilon)


def dot_nt(a, b):
    return lax.dot_general(a, b, (((1,), (1,)), ((), ())), preferred_element_type=jnp.float32)


def lane_sums(block):
    return jnp.sum(block.T, axis=0, keepdims=True)


def scale_kernel(z_ref, codes_ref, high_ref, low_ref):
    half, width = high_ref.shape
    codes = codes_ref[pl.ds(pl.multiple_of(z_ref[0] * half, half), half)]
    high, low = split(unit_rows(codes) * (inverse_temp / width))
    high_ref[...] = high
    low_ref[...] = low


def chunk_kernel(high_ref, low_ref, items_ref, out_ref, sums_ref, xh_ref, xl_ref, held_ref, sems):
    codes, step = high_ref.shape[0], 256
    total = items_ref.shape[0]
    edges = [0, step, total // 2, total]
    copies = [
        pltpu.make_async_copy(items_ref.at[pl.ds(a, b - a)], held_ref.at[pl.ds(a, b - a)], sems.at[i])
        for i, (a, b) in enumerate(zip(edges, edges[1:]))
    ]
    for copy in copies:
        copy.start()
    folded = [jnp.zeros((step, LANES), jnp.float32) for _ in range(0, codes, step)]
    for copy, begin, end in zip(copies, edges, edges[1:]):
        copy.wait()
        for first in range(begin, end, step):
            values = held_ref[first:first + step]
            xh_ref[first:first + step], xl_ref[first:first + step] = split(values)
            item_high, item_low = split(unit_rows(values))
            for k, start in enumerate(range(0, codes, step)):
                code_high = high_ref[start:start + step]
                code_low = low_ref[start:start + step]
                logits = dot_nt(code_high, item_high) + (dot_nt(code_high, item_low) + dot_nt(code_low, item_high))
                values = jnp.exp(logits)
                out_ref[start:start + step, first:first + step] = values
                for lane in range(0, step, LANES):
                    folded[k] = folded[k] + values[:, lane:lane + LANES]
    for k, total in enumerate(folded):
        for part in range(step // LANES):
            row = k * (step // LANES) + part
            sums_ref[row:row + 1] = lane_sums(total[part * LANES:(part + 1) * LANES])


def load_blocks(refs):
    return [(ref, j * LANES) for ref in refs for j in range(ref.shape[1] // LANES)]


def row_kernel(got_ref, *refs):
    blocks, out_ref = load_blocks(refs[:-1]), refs[-1]
    scale = 1.0 / (K * jnp.sum(got_ref[...], axis=0))
    totals = [jnp.zeros((SUB, LANES), jnp.float32) for _ in blocks]
    for b in range(scale.shape[0]):
        column = jnp.broadcast_to(scale[b:b + 1], (LANES, LANES)).T
        for j, (ref, lane) in enumerate(blocks):
            product = ref[b * LANES:(b + 1) * LANES, lane:lane + LANES] * column
            totals[j] = totals[j] + jnp.sum(product.reshape(LANES // SUB, SUB, LANES), axis=0)
    sums = [jnp.sum(total, axis=0, keepdims=True) for total in totals]
    tile = jnp.concatenate(sums, axis=0)
    for peer in range(out_ref.shape[0]):
        out_ref[peer] = tile


def row_scales(total_items, got_ref):
    scale = 1.0 / (total_items * jnp.sum(got_ref[...], axis=0))
    return [scale[row:row + 1] for row in range(scale.shape[0])]


def col_kernel(total_items, got_ref, *refs):
    blocks, out_ref = load_blocks(refs[:-1]), refs[-1]
    scales = row_scales(total_items, got_ref)
    rows = []
    for b in range(out_ref.shape[1]):
        folded = jnp.zeros((LANES, LANES), jnp.float32)
        for (ref, lane), scale in zip(blocks, scales):
            folded = folded + ref[b * LANES:(b + 1) * LANES, lane:lane + LANES] * scale
        rows.append(lane_sums(folded))
    tile = jnp.concatenate(rows, axis=0)
    for peer in range(out_ref.shape[0]):
        out_ref[peer] = tile


def numer_kernel(total_items, count, nx, near, cores, got_ref, *refs):
    high_refs, low_refs, out_ref = refs[count:2 * count], refs[2 * count:3 * count], refs[3 * count]
    scales = row_scales(total_items, got_ref)
    codes, width = refs[0].shape[0], high_refs[0].shape[1]
    parts = codes // LANES
    per_x = width // (nx * SUB)
    step = 256
    mass = []
    for start in range(0, codes, step):
        folded = jnp.zeros((step, LANES), jnp.float32)
        sums, at = None, 0
        for ref, xh_ref, xl_ref in zip(refs[:count], high_refs, low_refs):
            highs, lows = [], []
            for lane in range(0, ref.shape[1], LANES):
                weights = ref[start:start + step, lane:lane + LANES] * scales[at]
                folded = folded + weights
                high, low = split(weights)
                highs.append(high)
                lows.append(low)
                at += 1
            high, low = jnp.concatenate(highs, axis=1), jnp.concatenate(lows, axis=1)
            xh, xl = xh_ref[...], xl_ref[...]
            more = jnp.dot(high, xh, preferred_element_type=jnp.float32) + (
                jnp.dot(low, xh, preferred_element_type=jnp.float32)
                + jnp.dot(high, xl, preferred_element_type=jnp.float32)
            )
            sums = more if sums is None else sums + more
        for part in range(step // LANES):
            mass.append(lane_sums(folded[part * LANES:(part + 1) * LANES]))
            col = start // LANES + part
            for lane in range(0, width, LANES):
                turned = sums[part * LANES:(part + 1) * LANES, lane:lane + LANES].T
                for group in range(LANES // SUB):
                    x, rest = divmod(lane // SUB + group, per_x)
                    y, core = divmod(rest, cores)
                    row = core * (per_x // (near * cores)) + y // near
                    out_ref[(y % near) * nx + x, row * parts + col] = turned[group * SUB:(group + 1) * SUB]
    tile = jnp.concatenate(mass + [jnp.ones((SUB - parts, LANES), jnp.float32)], axis=0)
    for peer in range(out_ref.shape[0]):
        out_ref[peer, out_ref.shape[1] - 1] = tile


def repack_kernel(got_ref, out_ref):
    summed = got_ref[0]
    for x in range(1, got_ref.shape[0]):
        summed = summed + got_ref[x]
    peers, count = out_ref.shape[0], out_ref.shape[1] - 1
    for peer in range(peers):
        out_ref[peer, :count] = summed[peer * count:(peer + 1) * count]
        out_ref[peer, count] = summed[peers * count]


def lookup_kernel(z_ref, index_ref, codes_ref, out_ref):
    part0 = codes_ref[...].astype(jnp.bfloat16)
    rest = codes_ref[...] - part0.astype(jnp.float32)
    part1 = rest.astype(jnp.bfloat16)
    part2 = (rest - part1.astype(jnp.float32)).astype(jnp.bfloat16)
    codes = codes_ref.shape[0]
    for block in range(out_ref.shape[0] // LANES):
        local = index_ref[block:block + 1] - z_ref[1]
        column = jnp.broadcast_to(local.astype(jnp.float32), (LANES, LANES)).T
        hits = []
        for b in range(codes // LANES):
            lane = lax.broadcasted_iota(jnp.int32, (LANES, LANES), 1) + b * LANES
            hits.append(jnp.where(column == lane.astype(jnp.float32), 1.0, 0.0).astype(jnp.bfloat16))
        chosen = jnp.concatenate(hits, axis=1)
        found = jnp.dot(chosen, part2, preferred_element_type=jnp.float32)
        found = jnp.dot(chosen, part1, preferred_element_type=jnp.float32) + found
        found = jnp.dot(chosen, part0, preferred_element_type=jnp.float32) + found
        out_ref[block * LANES:(block + 1) * LANES] = found


def finish_kernel(cores, got_ref, items_ref, looked_ref, out_ref, residual_ref):
    residual_ref[...] = items_ref[...] - looked_ref[...]
    peers, parts = got_ref.shape[0], got_ref.shape[1] - 1
    for core in range(cores):
        first = core * (peers // cores)
        summed = got_ref[first]
        for peer in range(first + 1, first + peers // cores):
            summed = summed + got_ref[peer]
        for b in range(parts):
            lane = (core * parts + b) * LANES
            out_ref[:, lane:lane + LANES] = summed[b] / summed[parts][b:b + 1]


def body(items, codewords, assign):
    f32 = jnp.float32
    n = lax.axis_size("code")
    nx, nc = lax.axis_size("x"), lax.axis_size("core")
    high, low = lax.axis_size("yh"), lax.axis_size("yl")
    ny = high * low
    local_codes, width = codewords.shape
    own_rows = items.shape[0]
    half = local_codes // nc
    total_items = own_rows * nc * n * nx * ny
    core = lax.axis_index("core")
    z_info = jnp.stack([core, lax.axis_index("code") * local_codes]).astype(jnp.int32)

    gathered = lax.all_gather(items, ("core", "code"), axis=0, tiled=True)
    scaled = jax.ShapeDtypeStruct((half, width), jnp.bfloat16)
    code_high, code_low = call(scale_kernel, (scaled, scaled), [SMEM, VMEM])(z_info, codewords)
    index_tile = assign.reshape(-1, LANES)
    named = call(lookup_kernel, jax.ShapeDtypeStruct((assign.shape[0], width), f32), [SMEM, VMEM, VMEM], grant=12)(
        z_info, index_tile, codewords
    )
    gathered, named, code_high, code_low = lax.optimization_barrier((gathered, named, code_high, code_low))
    looked = lax.psum_scatter(named, "code", scatter_dimension=0, tiled=True)
    group = gathered.shape[0]
    part = jax.ShapeDtypeStruct((group, width), jnp.bfloat16)
    kernel_vals, col_tile, item_high, item_low = call(
        chunk_kernel,
        (
            jax.ShapeDtypeStruct((half, group), f32),
            jax.ShapeDtypeStruct((half // LANES, LANES), f32),
            part,
            part,
        ),
        [VMEM, VMEM, pl.BlockSpec(memory_space=pl.ANY)],
        [pltpu.VMEM((group, width), f32), pltpu.SemaphoreType.DMA((3,))],
        grant=16,
    )(code_high, code_low, pltpu.with_memory_space_constraint(gathered, pltpu.HBM))
    blocks, count = [kernel_vals], 1

    row_shape = jax.ShapeDtypeStruct((nc * n, nc * n, LANES), f32)
    col_shape = jax.ShapeDtypeStruct((nx * ny,) + col_tile.shape, f32)
    operands = [VMEM] * (1 + count)
    cols = jnp.broadcast_to(col_tile[None], col_shape.shape)
    for turn in range(ITERS):
        got = lax.all_to_all(cols, ("yh", "yl", "x"), 0, 0)
        rows = call(row_kernel, row_shape, operands)(got, *blocks)
        got = lax.all_to_all(rows, ("core", "code"), 0, 0)
        if turn < ITERS - 1:
            cols = call(functools.partial(col_kernel, total_items), col_shape, operands)(got, *blocks)

    per_owner = width // (nx * ny * nc)
    tiles = high * nc * (per_owner // SUB) * (half // LANES)
    numer = call(
        functools.partial(numer_kernel, total_items, count, nx, low, nc),
        jax.ShapeDtypeStruct((nx * low, tiles + 1, SUB, LANES), f32),
        operands + [VMEM] * (2 * count),
        grant=16,
    )(got, *blocks, item_high, item_low)
    numer, looked = lax.optimization_barrier((numer, looked))
    got = lax.all_to_all(numer, ("yl", "x"), 0, 0)
    peers = high * nc
    packed = call(repack_kernel, jax.ShapeDtypeStruct((peers, tiles // peers + 1, SUB, LANES), f32), [VMEM])(got)
    got = lax.all_to_all(packed, ("core", "yh"), 0, 0)
    shapes = (jax.ShapeDtypeStruct((per_owner, local_codes), f32), jax.ShapeDtypeStruct(items.shape, f32))
    turned, residual = call(functools.partial(finish_kernel, nc), shapes, [VMEM] * 3)(got, items, looked)
    new_codewords = turned.T
    return (new_codewords, residual)


def solution(mesh):
    cores = 2
    high, low = 4, 2
    dp, code = mesh.devices.shape
    fine = Mesh(
        mesh.devices.reshape(dp // (high * low * cores), high, low, cores, code),
        ("x", "yh", "yl", "core", "code"),
    )
    in_specs = (P(DP + ("code",), None), P("code", None), P(DP))
    out_specs = (P("code", DP), P(DP + ("code",), None))
    return jax.shard_map(body, mesh=fine, in_specs=in_specs, out_specs=out_specs, check_vma=False)
```

```python
import functools

import jax
import jax.numpy as jnp
from jax import lax
from jax.experimental import pallas as pl
from jax.experimental.pallas import tpu as pltpu
from jax.sharding import Mesh, PartitionSpec as P

K = 8192
ITERS = 3
DP = ("x", "yh", "yl", "core")
LANES = 128
SUB = 8

epsilon = 1e-05
inverse_temp = 64.0

VMEM = pl.BlockSpec(memory_space=pltpu.VMEM)
SMEM = pl.BlockSpec(memory_space=pltpu.SMEM)
MIB = 1024 * 1024


def call(body, out_shape, ins, scratch=(), grant=8):
    return pl.pallas_call(
        body,
        out_shape=out_shape,
        in_specs=ins,
        out_specs=jax.tree.map(lambda _: VMEM, out_shape),
        scratch_shapes=list(scratch),
        compiler_params=pltpu.CompilerParams(vmem_limit_bytes=grant * MIB),
    )


def split(values):
    high = values.astype(jnp.bfloat16)
    return high, (values - high.astype(jnp.float32)).astype(jnp.bfloat16)


def unit_rows(values):
    return values * lax.rsqrt(jnp.mean(values * values, axis=-1, keepdims=True) + epsilon)


def dot_nt(a, b):
    return lax.dot_general(a, b, (((1,), (1,)), ((), ())), preferred_element_type=jnp.float32)


def lane_sums(block):
    return jnp.sum(block.T, axis=0, keepdims=True)


def scale_kernel(z_ref, codes_ref, high_ref, low_ref):
    half, width = high_ref.shape
    codes = codes_ref[pl.ds(pl.multiple_of(z_ref[0] * half, half), half)]
    high, low = split(unit_rows(codes) * (inverse_temp / width))
    high_ref[...] = high
    low_ref[...] = low


def chunk_kernel(high_ref, low_ref, items_ref, out_ref, sums_ref, xh_ref, xl_ref, held_ref, sems):
    codes, step = high_ref.shape[0], 256
    total = items_ref.shape[0]
    edges = [0, step, 2 * step, total // 2, total]
    copies = [
        pltpu.make_async_copy(items_ref.at[pl.ds(a, b - a)], held_ref.at[pl.ds(a, b - a)], sems.at[i])
        for i, (a, b) in enumerate(zip(edges, edges[1:]))
    ]
    for copy in copies:
        copy.start()
    code_high, code_low = high_ref[...], low_ref[...]
    folded = jnp.zeros((codes, LANES), jnp.float32)
    for copy, begin, end in zip(copies, edges, edges[1:]):
        copy.wait()
        for first in range(begin, end, step):
            values = held_ref[first:first + step]
            xh_ref[first:first + step], xl_ref[first:first + step] = split(values)
            item_high, item_low = split(unit_rows(values))
            logits = dot_nt(code_high, item_high) + (dot_nt(code_high, item_low) + dot_nt(code_low, item_high))
            values = jnp.exp(logits)
            out_ref[:, first:first + step] = values
            for lane in range(0, step, LANES):
                folded = folded + values[:, lane:lane + LANES]
    for row in range(codes // LANES):
        sums_ref[row:row + 1] = lane_sums(folded[row * LANES:(row + 1) * LANES])


def load_blocks(refs):
    return [(ref, j * LANES) for ref in refs for j in range(ref.shape[1] // LANES)]


def row_kernel(got_ref, *refs):
    blocks, out_ref = load_blocks(refs[:-1]), refs[-1]
    scale = 1.0 / (K * jnp.sum(got_ref[...], axis=0))
    totals = [jnp.zeros((SUB, LANES), jnp.float32) for _ in blocks]
    for b in range(scale.shape[0]):
        column = jnp.broadcast_to(scale[b:b + 1], (LANES, LANES)).T
        for j, (ref, lane) in enumerate(blocks):
            product = ref[b * LANES:(b + 1) * LANES, lane:lane + LANES] * column
            totals[j] = totals[j] + jnp.sum(product.reshape(LANES // SUB, SUB, LANES), axis=0)
    sums = [jnp.sum(total, axis=0, keepdims=True) for total in totals]
    tile = jnp.concatenate(sums, axis=0)
    for peer in range(out_ref.shape[0]):
        out_ref[peer] = tile


def row_scales(total_items, got_ref):
    scale = 1.0 / (total_items * jnp.sum(got_ref[...], axis=0))
    return [scale[row:row + 1] for row in range(scale.shape[0])]


def col_kernel(total_items, got_ref, *refs):
    blocks, out_ref = load_blocks(refs[:-1]), refs[-1]
    scales = row_scales(total_items, got_ref)
    rows = []
    for b in range(out_ref.shape[1]):
        folded = jnp.zeros((LANES, LANES), jnp.float32)
        for (ref, lane), scale in zip(blocks, scales):
            folded = folded + ref[b * LANES:(b + 1) * LANES, lane:lane + LANES] * scale
        rows.append(lane_sums(folded))
    tile = jnp.concatenate(rows, axis=0)
    for peer in range(out_ref.shape[0]):
        out_ref[peer] = tile


def numer_kernel(total_items, count, nx, near, cores, got_ref, *refs):
    high_refs, low_refs, out_ref = refs[count:2 * count], refs[2 * count:3 * count], refs[3 * count]
    scales = row_scales(total_items, got_ref)
    codes, width = refs[0].shape[0], high_refs[0].shape[1]
    parts = codes // LANES
    per_x = width // (nx * SUB)
    step = codes
    mass = []
    for start in range(0, codes, step):
        folded = jnp.zeros((step, LANES), jnp.float32)
        sums, at = None, 0
        for ref, xh_ref, xl_ref in zip(refs[:count], high_refs, low_refs):
            for first in range(0, ref.shape[1], 512):
                highs, lows = [], []
                for lane in range(first, first + 512, LANES):
                    weights = ref[start:start + step, lane:lane + LANES] * scales[at]
                    folded = folded + weights
                    high, low = split(weights)
                    highs.append(high)
                    lows.append(low)
                    at += 1
                high, low = jnp.concatenate(highs, axis=1), jnp.concatenate(lows, axis=1)
                xh, xl = xh_ref[first:first + 512], xl_ref[first:first + 512]
                more = jnp.dot(high, xh, preferred_element_type=jnp.float32) + (
                    jnp.dot(low, xh, preferred_element_type=jnp.float32)
                    + jnp.dot(high, xl, preferred_element_type=jnp.float32)
                )
                sums = more if sums is None else sums + more
        for part in range(step // LANES):
            mass.append(lane_sums(folded[part * LANES:(part + 1) * LANES]))
            col = start // LANES + part
            for lane in range(0, width, LANES):
                turned = sums[part * LANES:(part + 1) * LANES, lane:lane + LANES].T
                for group in range(LANES // SUB):
                    x, rest = divmod(lane // SUB + group, per_x)
                    y, core = divmod(rest, cores)
                    row = core * (per_x // (near * cores)) + y // near
                    out_ref[(y % near) * nx + x, row * parts + col] = turned[group * SUB:(group + 1) * SUB]
    tile = jnp.concatenate(mass + [jnp.ones((SUB - parts, LANES), jnp.float32)], axis=0)
    for peer in range(out_ref.shape[0]):
        out_ref[peer, out_ref.shape[1] - 1] = tile


def repack_kernel(got_ref, out_ref):
    summed = got_ref[0]
    for x in range(1, got_ref.shape[0]):
        summed = summed + got_ref[x]
    peers, count = out_ref.shape[0], out_ref.shape[1] - 1
    for peer in range(peers):
        out_ref[peer, :count] = summed[peer * count:(peer + 1) * count]
        out_ref[peer, count] = summed[peers * count]


def lookup_kernel(z_ref, index_ref, codes_ref, out_ref):
    part0 = codes_ref[...].astype(jnp.bfloat16)
    rest = codes_ref[...] - part0.astype(jnp.float32)
    part1 = rest.astype(jnp.bfloat16)
    part2 = (rest - part1.astype(jnp.float32)).astype(jnp.bfloat16)
    codes = codes_ref.shape[0]
    for block in range(out_ref.shape[0] // LANES):
        local = index_ref[block:block + 1] - z_ref[1]
        column = jnp.broadcast_to(local.astype(jnp.float32), (LANES, LANES)).T
        hits = []
        for b in range(codes // LANES):
            lane = lax.broadcasted_iota(jnp.int32, (LANES, LANES), 1) + b * LANES
            hits.append(jnp.where(column == lane.astype(jnp.float32), 1.0, 0.0).astype(jnp.bfloat16))
        chosen = jnp.concatenate(hits, axis=1)
        found = jnp.dot(chosen, part2, preferred_element_type=jnp.float32)
        found = jnp.dot(chosen, part1, preferred_element_type=jnp.float32) + found
        found = jnp.dot(chosen, part0, preferred_element_type=jnp.float32) + found
        out_ref[block * LANES:(block + 1) * LANES] = found


def finish_kernel(cores, got_ref, items_ref, looked_ref, out_ref, residual_ref):
    residual_ref[...] = items_ref[...] - looked_ref[...]
    peers, parts = got_ref.shape[0], got_ref.shape[1] - 1
    for core in range(cores):
        first = core * (peers // cores)
        summed = got_ref[first]
        for peer in range(first + 1, first + peers // cores):
            summed = summed + got_ref[peer]
        for b in range(parts):
            lane = (core * parts + b) * LANES
            out_ref[:, lane:lane + LANES] = summed[b] / summed[parts][b:b + 1]


def body(items, codewords, assign):
    f32 = jnp.float32
    n = lax.axis_size("code")
    nx, nc = lax.axis_size("x"), lax.axis_size("core")
    high, low = lax.axis_size("yh"), lax.axis_size("yl")
    ny = high * low
    local_codes, width = codewords.shape
    own_rows = items.shape[0]
    half = local_codes // nc
    total_items = own_rows * nc * n * nx * ny
    core = lax.axis_index("core")
    z_info = jnp.stack([core, lax.axis_index("code") * local_codes]).astype(jnp.int32)

    gathered = lax.all_gather(items, ("core", "code"), axis=0, tiled=True)
    scaled = jax.ShapeDtypeStruct((half, width), jnp.bfloat16)
    code_high, code_low = call(scale_kernel, (scaled, scaled), [SMEM, VMEM])(z_info, codewords)
    index_tile = assign.reshape(-1, LANES)
    named = call(lookup_kernel, jax.ShapeDtypeStruct((assign.shape[0], width), f32), [SMEM, VMEM, VMEM], grant=12)(
        z_info, index_tile, codewords
    )
    gathered, named, code_high, code_low = lax.optimization_barrier((gathered, named, code_high, code_low))
    looked = lax.psum_scatter(named, "code", scatter_dimension=0, tiled=True)
    group = gathered.shape[0]
    part = jax.ShapeDtypeStruct((group, width), jnp.bfloat16)
    kernel_vals, col_tile, item_high, item_low = call(
        chunk_kernel,
        (
            jax.ShapeDtypeStruct((half, group), f32),
            jax.ShapeDtypeStruct((half // LANES, LANES), f32),
            part,
            part,
        ),
        [VMEM, VMEM, pl.BlockSpec(memory_space=pl.ANY)],
        [pltpu.VMEM((group, width), f32), pltpu.SemaphoreType.DMA((4,))],
        grant=16,
    )(code_high, code_low, pltpu.with_memory_space_constraint(gathered, pltpu.HBM))
    blocks, count = [kernel_vals], 1

    row_shape = jax.ShapeDtypeStruct((nc * n, nc * n, LANES), f32)
    col_shape = jax.ShapeDtypeStruct((nx * ny,) + col_tile.shape, f32)
    operands = [VMEM] * (1 + count)
    cols = jnp.broadcast_to(col_tile[None], col_shape.shape)
    for turn in range(ITERS):
        got = lax.all_to_all(cols, ("yh", "yl", "x"), 0, 0)
        rows = call(row_kernel, row_shape, operands)(got, *blocks)
        got = lax.all_to_all(rows, ("core", "code"), 0, 0)
        if turn < ITERS - 1:
            cols = call(functools.partial(col_kernel, total_items), col_shape, operands)(got, *blocks)

    per_owner = width // (nx * ny * nc)
    tiles = high * nc * (per_owner // SUB) * (half // LANES)
    numer = call(
        functools.partial(numer_kernel, total_items, count, nx, low, nc),
        jax.ShapeDtypeStruct((nx * low, tiles + 1, SUB, LANES), f32),
        operands + [VMEM] * (2 * count),
        grant=16,
    )(got, *blocks, item_high, item_low)
    numer, looked = lax.optimization_barrier((numer, looked))
    got = lax.all_to_all(numer, ("yl", "x"), 0, 0)
    peers = high * nc
    packed = call(repack_kernel, jax.ShapeDtypeStruct((peers, tiles // peers + 1, SUB, LANES), f32), [VMEM])(got)
    got = lax.all_to_all(packed, ("core", "yh"), 0, 0)
    shapes = (jax.ShapeDtypeStruct((per_owner, local_codes), f32), jax.ShapeDtypeStruct(items.shape, f32))
    turned, residual = call(functools.partial(finish_kernel, nc), shapes, [VMEM] * 3)(got, items, looked)
    new_codewords = turned.T
    return (new_codewords, residual)


def solution(mesh):
    cores = 2
    high, low = 4, 2
    dp, code = mesh.devices.shape
    fine = Mesh(
        mesh.devices.reshape(dp // (high * low * cores), high, low, cores, code),
        ("x", "yh", "yl", "core", "code"),
    )
    in_specs = (P(DP + ("code",), None), P("code", None), P(DP))
    out_specs = (P("code", DP), P(DP + ("code",), None))
    return jax.shard_map(body, mesh=fine, in_specs=in_specs, out_specs=out_specs, check_vma=False)
```

```python
import functools

import jax
import jax.numpy as jnp
from jax import lax
from jax.experimental import pallas as pl
from jax.experimental.pallas import tpu as pltpu
from jax.sharding import Mesh, PartitionSpec as P

K = 8192
ITERS = 3
DP = ("x", "yh", "yl", "core")
LANES = 128
SUB = 8

epsilon = 1e-05
inverse_temp = 64.0
LOG2_E = 1.4426950408889634

VMEM = pl.BlockSpec(memory_space=pltpu.VMEM)
SMEM = pl.BlockSpec(memory_space=pltpu.SMEM)
MIB = 1024 * 1024


def call(body, out_shape, ins, scratch=(), grant=8):
    return pl.pallas_call(
        body,
        out_shape=out_shape,
        in_specs=ins,
        out_specs=jax.tree.map(lambda _: VMEM, out_shape),
        scratch_shapes=list(scratch),
        compiler_params=pltpu.CompilerParams(vmem_limit_bytes=grant * MIB),
    )


def split(values):
    high = values.astype(jnp.bfloat16)
    return high, (values - high.astype(jnp.float32)).astype(jnp.bfloat16)


def unit_rows(values):
    return values * lax.rsqrt(jnp.mean(values * values, axis=-1, keepdims=True) + epsilon)


def dot_nt(a, b):
    return lax.dot_general(a, b, (((1,), (1,)), ((), ())), preferred_element_type=jnp.float32)


def lane_sums(block):
    return jnp.sum(block.T, axis=0, keepdims=True)


def scale_kernel(z_ref, codes_ref, high_ref, low_ref):
    half, width = high_ref.shape
    codes = codes_ref[pl.ds(pl.multiple_of(z_ref[0] * half, half), half)]
    high, low = split(unit_rows(codes) * (inverse_temp / width * LOG2_E))
    high_ref[...] = high
    low_ref[...] = low


def chunk_kernel(high_ref, low_ref, items_ref, out_ref, sums_ref, xh_ref, xl_ref, norm_ref, held_ref, sems):
    codes, step = high_ref.shape[0], 256
    total = items_ref.shape[0]
    edges = [0, step, total // 2, total]
    copies = [
        pltpu.make_async_copy(items_ref.at[pl.ds(a, b - a)], held_ref.at[pl.ds(a, b - a)], sems.at[i])
        for i, (a, b) in enumerate(zip(edges, edges[1:]))
    ]
    for copy in copies:
        copy.start()
    folded = [jnp.zeros((step, LANES), jnp.float32) for _ in range(0, codes, step)]
    for copy, begin, end in zip(copies, edges, edges[1:]):
        copy.wait()
        for first in range(begin, end, step):
            values = held_ref[first:first + step]
            power = jnp.mean(values * values, axis=-1, keepdims=True) + epsilon
            inverse = lax.rsqrt(power)
            item_high, item_low = split(values * inverse)
            xh_ref[first:first + step], xl_ref[first:first + step] = item_high, item_low
            norm = power * inverse
            for at in range(0, step, LANES):
                row = (first + at) // LANES
                norm_ref[row:row + 1] = jnp.broadcast_to(norm[at:at + LANES], (LANES, LANES)).T[:1]
            for k, start in enumerate(range(0, codes, step)):
                code_high = high_ref[start:start + step]
                code_low = low_ref[start:start + step]
                logits = dot_nt(code_high, item_high) + (dot_nt(code_high, item_low) + dot_nt(code_low, item_high))
                values = jnp.exp2(logits)
                out_ref[start:start + step, first:first + step] = values
                for lane in range(0, step, LANES):
                    folded[k] = folded[k] + values[:, lane:lane + LANES]
    for k, total in enumerate(folded):
        for part in range(step // LANES):
            row = k * (step // LANES) + part
            sums_ref[row:row + 1] = lane_sums(total[part * LANES:(part + 1) * LANES])


def load_blocks(refs):
    return [(ref, j * LANES) for ref in refs for j in range(ref.shape[1] // LANES)]


def row_kernel(got_ref, *refs):
    blocks, out_ref = load_blocks(refs[:-1]), refs[-1]
    scale = 1.0 / (K * jnp.sum(got_ref[...], axis=0))
    totals = [jnp.zeros((SUB, LANES), jnp.float32) for _ in blocks]
    for b in range(scale.shape[0]):
        column = jnp.broadcast_to(scale[b:b + 1], (LANES, LANES)).T
        for j, (ref, lane) in enumerate(blocks):
            product = ref[b * LANES:(b + 1) * LANES, lane:lane + LANES] * column
            totals[j] = totals[j] + jnp.sum(product.reshape(LANES // SUB, SUB, LANES), axis=0)
    sums = [jnp.sum(total, axis=0, keepdims=True) for total in totals]
    tile = jnp.concatenate(sums, axis=0)
    for peer in range(out_ref.shape[0]):
        out_ref[peer] = tile


def row_scales(total_items, got_ref):
    scale = 1.0 / (total_items * jnp.sum(got_ref[...], axis=0))
    return [scale[row:row + 1] for row in range(scale.shape[0])]


def col_kernel(total_items, got_ref, *refs):
    blocks, out_ref = load_blocks(refs[:-1]), refs[-1]
    scales = row_scales(total_items, got_ref)
    rows = []
    for b in range(out_ref.shape[1]):
        folded = jnp.zeros((LANES, LANES), jnp.float32)
        for (ref, lane), scale in zip(blocks, scales):
            folded = folded + ref[b * LANES:(b + 1) * LANES, lane:lane + LANES] * scale
        rows.append(lane_sums(folded))
    tile = jnp.concatenate(rows, axis=0)
    for peer in range(out_ref.shape[0]):
        out_ref[peer] = tile


def numer_kernel(total_items, count, nx, near, cores, got_ref, norm_ref, *refs):
    high_refs, low_refs, out_ref = refs[count:2 * count], refs[2 * count:3 * count], refs[3 * count]
    scales = row_scales(total_items, got_ref)
    codes, width = refs[0].shape[0], high_refs[0].shape[1]
    parts = codes // LANES
    per_x = width // (nx * SUB)
    step = 256
    mass = []
    for start in range(0, codes, step):
        folded = jnp.zeros((step, LANES), jnp.float32)
        sums, at = None, 0
        for ref, xh_ref, xl_ref in zip(refs[:count], high_refs, low_refs):
            highs, lows = [], []
            for lane in range(0, ref.shape[1], LANES):
                weights = ref[start:start + step, lane:lane + LANES] * scales[at]
                folded = folded + weights
                high, low = split(weights * norm_ref[at:at + 1])
                highs.append(high)
                lows.append(low)
                at += 1
            high, low = jnp.concatenate(highs, axis=1), jnp.concatenate(lows, axis=1)
            xh, xl = xh_ref[...], xl_ref[...]
            more = jnp.dot(high, xh, preferred_element_type=jnp.float32) + (
                jnp.dot(low, xh, preferred_element_type=jnp.float32)
                + jnp.dot(high, xl, preferred_element_type=jnp.float32)
            )
            sums = more if sums is None else sums + more
        for part in range(step // LANES):
            mass.append(lane_sums(folded[part * LANES:(part + 1) * LANES]))
            col = start // LANES + part
            for lane in range(0, width, LANES):
                turned = sums[part * LANES:(part + 1) * LANES, lane:lane + LANES].T
                for group in range(LANES // SUB):
                    x, rest = divmod(lane // SUB + group, per_x)
                    y, core = divmod(rest, cores)
                    row = core * (per_x // (near * cores)) + y // near
                    out_ref[(y % near) * nx + x, row * parts + col] = turned[group * SUB:(group + 1) * SUB]
    tile = jnp.concatenate(mass + [jnp.ones((SUB - parts, LANES), jnp.float32)], axis=0)
    for peer in range(out_ref.shape[0]):
        out_ref[peer, out_ref.shape[1] - 1] = tile


def repack_kernel(got_ref, out_ref):
    summed = got_ref[0]
    for x in range(1, got_ref.shape[0]):
        summed = summed + got_ref[x]
    peers, count = out_ref.shape[0], out_ref.shape[1] - 1
    for peer in range(peers):
        out_ref[peer, :count] = summed[peer * count:(peer + 1) * count]
        out_ref[peer, count] = summed[peers * count]


def lookup_kernel(z_ref, index_ref, codes_ref, out_ref):
    part0 = codes_ref[...].astype(jnp.bfloat16)
    rest = codes_ref[...] - part0.astype(jnp.float32)
    part1 = rest.astype(jnp.bfloat16)
    part2 = (rest - part1.astype(jnp.float32)).astype(jnp.bfloat16)
    codes = codes_ref.shape[0]
    for block in range(out_ref.shape[0] // LANES):
        local = index_ref[block:block + 1] - z_ref[1]
        column = jnp.broadcast_to(local.astype(jnp.float32), (LANES, LANES)).T
        hits = []
        for b in range(codes // LANES):
            lane = lax.broadcasted_iota(jnp.int32, (LANES, LANES), 1) + b * LANES
            hits.append(jnp.where(column == lane.astype(jnp.float32), 1.0, 0.0).astype(jnp.bfloat16))
        chosen = jnp.concatenate(hits, axis=1)
        found = jnp.dot(chosen, part2, preferred_element_type=jnp.float32)
        found = jnp.dot(chosen, part1, preferred_element_type=jnp.float32) + found
        found = jnp.dot(chosen, part0, preferred_element_type=jnp.float32) + found
        out_ref[block * LANES:(block + 1) * LANES] = found


def finish_kernel(cores, got_ref, items_ref, looked_ref, out_ref, residual_ref):
    residual_ref[...] = items_ref[...] - looked_ref[...]
    peers, parts = got_ref.shape[0], got_ref.shape[1] - 1
    for core in range(cores):
        first = core * (peers // cores)
        summed = got_ref[first]
        for peer in range(first + 1, first + peers // cores):
            summed = summed + got_ref[peer]
        for b in range(parts):
            lane = (core * parts + b) * LANES
            out_ref[:, lane:lane + LANES] = summed[b] / summed[parts][b:b + 1]


def body(items, codewords, assign):
    f32 = jnp.float32
    n = lax.axis_size("code")
    nx, nc = lax.axis_size("x"), lax.axis_size("core")
    high, low = lax.axis_size("yh"), lax.axis_size("yl")
    ny = high * low
    local_codes, width = codewords.shape
    own_rows = items.shape[0]
    half = local_codes // nc
    total_items = own_rows * nc * n * nx * ny
    core = lax.axis_index("core")
    z_info = jnp.stack([core, lax.axis_index("code") * local_codes]).astype(jnp.int32)

    gathered = lax.all_gather(items, ("core", "code"), axis=0, tiled=True)
    scaled = jax.ShapeDtypeStruct((half, width), jnp.bfloat16)
    code_high, code_low = call(scale_kernel, (scaled, scaled), [SMEM, VMEM])(z_info, codewords)
    index_tile = assign.reshape(-1, LANES)
    named = call(lookup_kernel, jax.ShapeDtypeStruct((assign.shape[0], width), f32), [SMEM, VMEM, VMEM], grant=12)(
        z_info, index_tile, codewords
    )
    gathered, named, code_high, code_low = lax.optimization_barrier((gathered, named, code_high, code_low))
    looked = lax.psum_scatter(named, "code", scatter_dimension=0, tiled=True)
    group = gathered.shape[0]
    part = jax.ShapeDtypeStruct((group, width), jnp.bfloat16)
    kernel_vals, col_tile, item_high, item_low, norms = call(
        chunk_kernel,
        (
            jax.ShapeDtypeStruct((half, group), f32),
            jax.ShapeDtypeStruct((half // LANES, LANES), f32),
            part,
            part,
            jax.ShapeDtypeStruct((group // LANES, LANES), f32),
        ),
        [VMEM, VMEM, pl.BlockSpec(memory_space=pl.ANY)],
        [pltpu.VMEM((group, width), f32), pltpu.SemaphoreType.DMA((3,))],
        grant=16,
    )(code_high, code_low, pltpu.with_memory_space_constraint(gathered, pltpu.HBM))
    blocks, count = [kernel_vals], 1

    row_shape = jax.ShapeDtypeStruct((nc * n, nc * n, LANES), f32)
    col_shape = jax.ShapeDtypeStruct((nx * ny,) + col_tile.shape, f32)
    operands = [VMEM] * (1 + count)
    cols = jnp.broadcast_to(col_tile[None], col_shape.shape)
    for turn in range(ITERS):
        got = lax.all_to_all(cols, ("yh", "yl", "x"), 0, 0)
        rows = call(row_kernel, row_shape, operands)(got, *blocks)
        got = lax.all_to_all(rows, ("core", "code"), 0, 0)
        if turn < ITERS - 1:
            cols = call(functools.partial(col_kernel, total_items), col_shape, operands)(got, *blocks)

    per_owner = width // (nx * ny * nc)
    tiles = high * nc * (per_owner // SUB) * (half // LANES)
    numer = call(
        functools.partial(numer_kernel, total_items, count, nx, low, nc),
        jax.ShapeDtypeStruct((nx * low, tiles + 1, SUB, LANES), f32),
        operands + [VMEM] * (1 + 2 * count),
        grant=16,
    )(got, norms, *blocks, item_high, item_low)
    numer, looked = lax.optimization_barrier((numer, looked))
    got = lax.all_to_all(numer, ("yl", "x"), 0, 0)
    peers = high * nc
    packed = call(repack_kernel, jax.ShapeDtypeStruct((peers, tiles // peers + 1, SUB, LANES), f32), [VMEM])(got)
    got = lax.all_to_all(packed, ("core", "yh"), 0, 0)
    shapes = (jax.ShapeDtypeStruct((per_owner, local_codes), f32), jax.ShapeDtypeStruct(items.shape, f32))
    turned, residual = call(functools.partial(finish_kernel, nc), shapes, [VMEM] * 3)(got, items, looked)
    new_codewords = turned.T
    return (new_codewords, residual)


def solution(mesh):
    cores = 2
    high, low = 4, 2
    dp, code = mesh.devices.shape
    fine = Mesh(
        mesh.devices.reshape(dp // (high * low * cores), high, low, cores, code),
        ("x", "yh", "yl", "core", "code"),
    )
    in_specs = (P(DP + ("code",), None), P("code", None), P(DP))
    out_specs = (P("code", DP), P(DP + ("code",), None))
    return jax.shard_map(body, mesh=fine, in_specs=in_specs, out_specs=out_specs, check_vma=False)
```
